512 devices in a mesh: wide: 256 (over x, z, y), narrow: 2 (over core).
Axes of the slice: x: 4, y: 4, z: 16, core: 2. Of those that a mesh axis runs over, the one named last changes fastest.
Arguments:
- loads: bfloat16 [256, 2, 64, 1024], P('wide', 'narrow'), may hold values from -30 to 30
- flexibility: bfloat16 [256, 2, 1024, 1024], P('wide', 'narrow'), may hold values from -1 to 6
- dirichlet: bfloat16 [256, 2, 1024, 1024], P('wide', 'narrow'), may hold values from -1 to 6
- modes: bfloat16 [256, 2, 32, 1024], P('wide', 'narrow'), may hold values from -0.75 to 0.75
- coarse_inverse: bfloat16 [8192, 8192], P('wide', 'narrow'), may hold values from -1 to 4
- mode_counts: int32 [2, 256], replicated, may hold values from 1 to 32, 4096 in all within a row
Outputs:
- multipliers: bfloat16 [256, 2, 64, 1024], P('wide', 'narrow')
- residual: bfloat16 [256, 2, 64, 1024], P('wide', 'narrow')
The draws below stay inside these ranges and needn't reach their ends.
Inputs may be any that keep to these rules, and one draw needn't show every extreme that they name: `mode_counts`: each row of this array is one grid column; the counts of each grid column sum to exactly 4096 in all, and the largest count of each grid column is exactly 32.
All inputs are finite; a program needn't handle non-finite values.
Results may differ from the reference program's by a relative error of at most 0.0087.
The reference program's roundings to bfloat16 on the way (of `disp`, `rounded`, `inner`, `smoothed`, `weights`, `coarse_values` and `picked`) count: a program that leaves them out, or rounds other values in their place, can miss the bound.
Values may be sent and summed in bfloat16 or wider, within the bound.
No kernel may reach another device: no remote copies, remote signals or barrier semaphores. Data moves between devices by JAX's collectives and lax.ppermute only.
A program may use at most 64 MiB of HBM per device.

```python
import math
import jax
import jax.numpy as jnp
import numpy as np
from jax import lax

B = 1024
LOADS = 64
MAXM = 32
ITERS = 2
ROWS = 256
COLS = 2
MCOL = 4096
NC = 8192


def spd_stack(key, diag_low, diag_high, off_scale):

    def one_block(block_index):
        sub_key = jax.random.fold_in(key, block_index)
        first_key, second_key = jax.random.split(sub_key)
        raw_noise = jax.random.normal(first_key, (B, B), jnp.float32)
        symmetric = (raw_noise + raw_noise.T) * (off_scale / math.sqrt(2.0 * B))
        diagonal = jax.random.uniform(second_key, (B,), jnp.float32, diag_low, diag_high)
        return (symmetric + jnp.diag(diagonal)).astype(jnp.bfloat16)
    blocks = lax.map(one_block, jnp.arange(ROWS * COLS))
    return blocks.reshape(ROWS, COLS, B, B)


def draw_flexibility(key, part):
    sub_key = jax.random.fold_in(key, 11)
    return spd_stack(sub_key, 1.5, 3.0, 0.6)


def draw_dirichlet(key, part):
    sub_key = jax.random.fold_in(key, 23)
    return spd_stack(sub_key, 1.5, 3.0, 0.6)


def draw_coarse_inverse(key, part):
    first_key, second_key = jax.random.split(jax.random.fold_in(key, 37))
    raw_noise = jax.random.normal(first_key, (NC, NC), jnp.float32)
    off_scale, low_end, high_end, partner_value = (0.4, 1.0, 2.0, 0.7)
    symmetric = (raw_noise + raw_noise.T) * (off_scale / math.sqrt(2.0 * NC))
    diagonal = jax.random.uniform(second_key, (NC,), jnp.float32, low_end, high_end)
    index_list = jnp.arange(NC, dtype=jnp.int32)
    partner_mask = jnp.logical_and(index_list[:, None] % MCOL == index_list[None, :] % MCOL, index_list[:, None] != index_list[None, :])
    partner_part = jnp.where(partner_mask, partner_value / (COLS - 1), 0.0).astype(jnp.float32)
    return (symmetric + partner_part + jnp.diag(diagonal)).astype(jnp.bfloat16)


def draw_loads(key, part):
    noise_key, scale_key = jax.random.split(jax.random.fold_in(key, 5))
    raw_noise = jnp.clip(jax.random.normal(noise_key, (ROWS, COLS, LOADS, B), jnp.float32), -4.0, 4.0)
    spread = jnp.exp(jax.random.uniform(scale_key, (ROWS, COLS, 1, 1), jnp.float32, 0.0, math.log(2.0)))
    ramp = 3.0 ** (jnp.arange(ROWS, dtype=jnp.float32) / max(ROWS - 1, 1))
    return (raw_noise * spread * ramp[:, None, None, None]).astype(jnp.bfloat16)


def block_levels(key, shape, cuts, least, top_value):
    loudness = 1.0
    for dim, shards_of in cuts:
        heights = jax.random.uniform(jax.random.fold_in(jax.random.fold_in(key, 6), dim), (shards_of,), jnp.float32, least / len(cuts), top_value / len(cuts))
        loudness = loudness * jnp.repeat(jnp.exp(heights), shape[dim] // shards_of).reshape((-1,) + (1,) * (len(shape) - 1 - dim))
    return loudness


def length_profile(number_of, total, most, lean):
    portions = [(1 << 20) // math.isqrt(grade ** lean) + 1 for grade in range(2, number_of + 1)]
    surplus, counts = total - most - (number_of - 1), [1] * (number_of - 1)
    while surplus > 0:
        candidates = [i for i in range(number_of - 1) if counts[i] < most]
        mass, remaining = sum([portions[i] for i in candidates]), surplus
        for i in candidates:
            extra = min(most - counts[i], max(1, remaining * portions[i] // mass), surplus)
            counts[i] = counts[i] + extra
            surplus = surplus - extra
    return np.array([most] + counts)


def ragged_sizes(own_key, amount, total, reach, lean):
    if amount == 2:
        one = jax.random.randint(own_key, (), max(1, total - reach), min(reach, total - 1) + 1)
        return jnp.stack([one, total - one])
    sizes = jnp.asarray(length_profile(amount, total, reach, lean), jnp.int32)
    couples = (amount - 1) // 2
    source_of, taker = sizes[1:1 + 2 * couples:2], sizes[2:2 + 2 * couples:2]
    margin = jnp.minimum(source_of - 1, reach - taker)
    passed = jax.random.randint(jax.random.fold_in(own_key, 1), (couples,), 0, 1 << 20) % (margin + 1)
    sizes = sizes.at[1:1 + 2 * couples:2].set(source_of - passed).at[2:2 + 2 * couples:2].set(taker + passed)
    return sizes[jax.random.permutation(jax.random.fold_in(own_key, 2), amount)]


def bell_draw(own_key, extent, scale, reach, shards=(), kind=jnp.bfloat16):
    loudness = block_levels(own_key, extent, shards, -0.22, 0.18) if shards else 1.0
    entries = jax.random.normal(own_key, extent, jnp.float32) * scale * loudness
    return jnp.minimum(jnp.maximum(entries, -reach), reach).astype(kind)


def setup_inputs(seed: int = 0) -> dict:
    splits = jax.random.split(jax.random.key(seed), 7)
    loads = draw_loads(jax.random.fold_in(splits[6], 71), 0)
    flexibility = draw_flexibility(jax.random.fold_in(splits[6], 71), 0)
    dirichlet = draw_dirichlet(jax.random.fold_in(splits[6], 71), 0)
    modes = bell_draw(splits[3], (ROWS, COLS, MAXM, B), 0.125, 0.75, ((0, 256), (1, 2)))
    coarse_inverse = draw_coarse_inverse(jax.random.fold_in(splits[6], 71), 0)
    mode_counts = jax.vmap(lambda own: ragged_sizes(own, ROWS, MCOL, MAXM, 2))(jax.random.split(splits[5], COLS)).reshape((COLS, ROWS)).astype(jnp.int32)
    return {"loads": loads, "flexibility": flexibility, "dirichlet": dirichlet, "modes": modes, "coarse_inverse": coarse_inverse, "mode_counts": mode_counts}


def jump_all(values):
    row_count, col_count, load_count, width = values.shape
    face_len = width // 4
    face_parts = values.astype(jnp.float32).reshape(row_count, col_count, load_count, 4, face_len)
    north_face = face_parts[:, :, :, 0]
    south_face = face_parts[:, :, :, 1]
    west_face = face_parts[:, :, :, 2]
    east_face = face_parts[:, :, :, 3]
    zero_row = jnp.zeros_like(north_face[:1])
    zero_col = jnp.zeros_like(north_face[:, :1])
    from_above = jnp.concatenate([zero_row, south_face[:-1]], axis=0)
    from_below = jnp.concatenate([north_face[1:], zero_row], axis=0)
    from_west = jnp.concatenate([zero_col, east_face[:, :-1]], axis=1)
    from_east = jnp.concatenate([west_face[:, 1:], zero_col], axis=1)
    nearby = jnp.stack([from_above, from_below, from_west, from_east], axis=3)
    return (face_parts - nearby).reshape(values.shape)


def block_products(values, blocks):
    def one_product(operands):
        return jnp.dot(operands[0], operands[1], preferred_element_type=jnp.float32)
    flat_values = values.reshape((-1,) + values.shape[2:])
    flat_blocks = blocks.reshape((-1,) + blocks.shape[2:])
    result = lax.map(one_product, (flat_values, flat_blocks))
    return result.reshape(values.shape[:2] + result.shape[1:])


def coarse_tables(mode_counts):
    end_points = jnp.cumsum(mode_counts, axis=1).astype(jnp.int32)
    starts = (end_points - mode_counts).astype(jnp.int32)
    position = jnp.arange(MCOL, dtype=jnp.int32)
    owner_row = jnp.sum((end_points[:, None, :] <= position[None, :, None]).astype(jnp.int32), axis=2)
    slot_index = owner_row * MAXM + position[None, :] - jnp.take_along_axis(starts, owner_row, axis=1)
    return starts, slot_index


def coarse_part(rounded, modes, coarse_inverse, mode_counts, starts, slot_index):
    row_count, col_count, load_count = rounded.shape[0], rounded.shape[1], rounded.shape[2]
    weights = block_products(rounded, jnp.swapaxes(modes, 2, 3)).astype(jnp.bfloat16)
    pieces = []
    for column in range(col_count):
        padded = jnp.transpose(weights[:, column], (1, 0, 2)).reshape(load_count, row_count * MAXM)
        pieces.append(jnp.take(padded, slot_index[column], axis=0 + 1))
    gathered = jnp.concatenate(pieces, axis=1)
    coarse_values = jnp.dot(gathered, coarse_inverse.T, preferred_element_type=jnp.float32).astype(jnp.bfloat16)
    rank_list = jnp.arange(MAXM, dtype=jnp.int32)
    column_base = (jnp.arange(col_count, dtype=jnp.int32) * MCOL)[:, None, None]
    own_index = jnp.minimum(column_base + starts[:, :, None] + rank_list, NC - 1).astype(jnp.int32)
    is_valid = rank_list < mode_counts[:, :, None]
    picked = jnp.take(coarse_values, own_index.reshape(-1), axis=1).reshape(load_count, col_count, row_count, MAXM)
    picked = jnp.where(is_valid[None], picked, jnp.zeros_like(picked))
    picked = jnp.transpose(picked, (2, 1, 0, 3))
    return block_products(picked, modes)


def reference(loads, flexibility, dirichlet, modes, coarse_inverse, mode_counts):
    starts, slot_index = coarse_tables(mode_counts)

    def precondition(values):
        rounded = values.astype(jnp.bfloat16)
        inner = jump_all(rounded).astype(jnp.bfloat16)
        smoothed = block_products(inner, dirichlet).astype(jnp.bfloat16)
        return jump_all(smoothed) + coarse_part(rounded, modes, coarse_inverse, mode_counts, starts, slot_index)

    def load_dot(left, right):
        return jnp.sum(left * right, axis=(0, 1, 3))

    disp = block_products(loads, flexibility).astype(jnp.bfloat16)
    residual = jump_all(disp)
    multipliers = jnp.zeros_like(residual)
    direction = precondition(residual)
    energy = load_dot(residual, direction)
    for step_number in range(ITERS):
        moved = jump_all(direction.astype(jnp.bfloat16)).astype(jnp.bfloat16)
        image = jump_all(block_products(moved, flexibility).astype(jnp.bfloat16))
        step_size = energy / load_dot(direction, image)
        multipliers = multipliers + step_size[:, None] * direction
        residual = residual - step_size[:, None] * image
        if step_number + 1 < ITERS:
            fresh_z = precondition(residual)
            fresh = load_dot(residual, fresh_z)
            direction = fresh_z + (fresh / energy)[:, None] * direction
            energy = fresh
    return multipliers.astype(jnp.bfloat16), residual.astype(jnp.bfloat16)
```

```python
import jax
import jax.numpy as jnp
from jax import lax
from jax.experimental import pallas as pl
from jax.experimental.pallas import tpu as pltpu
from jax.sharding import Mesh, PartitionSpec as P

ITERS = 2
XYZ = (4, 16, 4)
WIDE = ("x", "z", "y")
INTERPRET = False


def spread(values, axes):
    count = lax.axis_size(axes)
    copies = jnp.broadcast_to(values[None], (count,) + values.shape)
    return lax.all_to_all(copies, axes, 0, 0, tiled=False)


def gather_blocks(block):
    stage = spread(block, "z")
    stage = spread(stage, ("x", "y"))
    return stage.reshape((-1,) + block.shape)


def total(partial):
    stage = jnp.sum(spread(partial, ("x", "y", "c")), axis=0)
    return jnp.sum(spread(stage, "z"), axis=0)


def neighbours(values):
    load_count, width = values.shape
    face = width // 4
    rows = lax.axis_size(WIDE)
    column = lax.axis_index("c")
    down = [(i, i + 1) for i in range(rows - 1)]
    up = [(i + 1, i) for i in range(rows - 1)]
    north, south, west, east = (values[:, k * face : (k + 1) * face] for k in range(4))
    from_above = lax.ppermute(south, WIDE, down)
    from_below = lax.ppermute(north, WIDE, up)
    side = lax.ppermute(jnp.where(column == 0, east, west), "c", [(0, 1), (1, 0)])
    nothing = jnp.zeros_like(side)
    from_west = jnp.where(column == 1, side, nothing)
    from_east = jnp.where(column == 0, side, nothing)
    return jnp.concatenate([from_above, from_below, from_west, from_east], axis=1)


def jump(values):
    return values.astype(jnp.float32) - neighbours(values).astype(jnp.float32)


def pack(wide_rows):
    half = wide_rows.shape[0] // 2
    return jnp.concatenate([wide_rows[:half], wide_rows[half:]], axis=1)


def pad_kernel(first_ref, source_ref, block_ref, out_ref):
    rows, columns = block_ref.shape
    window = min(384, columns)
    chunks = out_ref.shape[1] // 128
    position = lax.broadcasted_iota(jnp.int32, (window, 128), 0)

    def step(chunk, carry):
        low = pl.multiple_of(first_ref[chunk] * 128, 128)
        part = block_ref[:, pl.ds(low, window)]
        target = pl.multiple_of(chunk * 128, 128)
        for half in range(2):
            hot = jnp.where(position == source_ref[half, chunk] - low, 1.0, 0.0).astype(jnp.bfloat16)
            chosen = jnp.dot(part, hot, preferred_element_type=jnp.float32)
            out_ref[half * rows : (half + 1) * rows, pl.ds(target, 128)] = chosen.astype(jnp.bfloat16)
        return carry

    lax.fori_loop(0, chunks, step, 0)


def padded_inverse(block, starts, counts):
    rows, columns = block.shape
    subdomains = counts.shape[0]
    slots = 32
    half_slots = slots // 2
    rank = jnp.arange(slots, dtype=jnp.int32)
    source = jnp.where(rank[None, :] < counts[:, None], starts[:, None] + rank[None, :], -1)
    chunks = subdomains * half_slots // 128
    source = source.reshape(subdomains, 2, half_slots).transpose(1, 0, 2).reshape(2, chunks, 1, 128)
    window = min(384, columns)
    first = jnp.minimum(starts.reshape(chunks, -1)[:, 0] // 128, (columns - window) // 128)
    return pl.pallas_call(
        pad_kernel,
        out_shape=jax.ShapeDtypeStruct((2 * rows, subdomains * half_slots), jnp.bfloat16),
        in_specs=[
            pl.BlockSpec(memory_space=pltpu.SMEM),
            pl.BlockSpec(memory_space=pltpu.VMEM),
            pl.BlockSpec(memory_space=pltpu.VMEM),
        ],
        out_specs=pl.BlockSpec(memory_space=pltpu.VMEM),
        interpret=INTERPRET,
        name="pad_inverse",
    )(first, source, block)


def product_kernel(padded_ref, blocks_ref, out_ref):
    nx, nz, ny = XYZ
    rows = padded_ref.shape[0] // 2
    length = nz * ny * blocks_ref.shape[1]
    result = jnp.zeros((2 * rows, 128), jnp.float32)
    for x in range(nx):
        order = [x * ny * nz + y * nz + z for z in range(nz) for y in range(ny)]
        part = jnp.concatenate([blocks_ref[p] for p in order], axis=0)
        result += jnp.dot(
            padded_ref[:, x * length : (x + 1) * length], part, preferred_element_type=jnp.float32
        )
    joined = result[:rows] + pltpu.roll(result[rows:], 64, 1)
    lane = lax.broadcasted_iota(jnp.int32, (rows // 2, 128), 1)
    out_ref[...] = jnp.where(lane < 64, joined[: rows // 2], pltpu.roll(joined[rows // 2 :], 64, 1))


def coarse_product(padded, blocks):
    return pl.pallas_call(
        product_kernel,
        out_shape=jax.ShapeDtypeStruct((padded.shape[0] // 4, 128), jnp.float32),
        interpret=INTERPRET,
        name="coarse_product",
    )(padded, blocks)


def lift_kernel(info_ref, low_ref, high_ref, modes_ref, out_ref):
    slots = modes_ref.shape[0]
    window = jnp.concatenate([low_ref[0], high_ref[0]], axis=0)
    rank = lax.broadcasted_iota(jnp.int32, (slots, slots), 0)
    column = lax.broadcasted_iota(jnp.int32, (slots, slots), 1)
    offset = info_ref[2] + rank
    row = (offset // 32) * 16 + offset % 16
    half = (offset // 16) % 2
    hit = jnp.logical_and(row == column, rank < info_ref[3])
    first = jnp.where(jnp.logical_and(hit, half == 0), 1.0, 0.0).astype(jnp.bfloat16)
    second = jnp.where(jnp.logical_and(hit, half == 1), 1.0, 0.0).astype(jnp.bfloat16)
    picked = jnp.dot(first, window, preferred_element_type=jnp.float32) + pltpu.roll(
        jnp.dot(second, window, preferred_element_type=jnp.float32), 64, 1
    )
    lifted = lax.dot_general(
        picked.astype(jnp.bfloat16),
        modes_ref[...],
        (((0,), (0,)), ((), ())),
        preferred_element_type=jnp.float32,
    )
    out_ref[...] = lifted[: out_ref.shape[0]]


def lift(info, blocks, modes):
    half_slots = blocks.shape[1]
    load_count = 64
    width = modes.shape[1]
    return pl.pallas_call(
        lift_kernel,
        out_shape=jax.ShapeDtypeStruct((load_count, width), jnp.float32),
        grid_spec=pltpu.PrefetchScalarGridSpec(
            num_scalar_prefetch=1,
            grid=(1,),
            in_specs=[
                pl.BlockSpec((1, half_slots, 128), lambda i, info: (info[0], 0, 0)),
                pl.BlockSpec((1, half_slots, 128), lambda i, info: (info[1], 0, 0)),
                pl.BlockSpec(modes.shape, lambda i, info: (0, 0)),
            ],
            out_specs=pl.BlockSpec((load_count, width), lambda i, info: (0, 0)),
        ),
        interpret=INTERPRET,
        name="lift",
    )(info, blocks, blocks, modes)


def shards(loads, flexibility, dirichlet, modes, coarse_inverse, mode_counts):
    local_loads = loads[0, 0]
    flex_block = flexibility[0, 0]
    precond_block = dirichlet[0, 0]
    mode_block = modes[0, 0]
    nx, nz, ny = XYZ
    rows = lax.axis_size(WIDE)
    row = lax.axis_index(WIDE)
    column = lax.axis_index("c")
    column_width = coarse_inverse.shape[1]
    width = local_loads.shape[1]
    face = width // 4

    counts = lax.dynamic_index_in_dim(mode_counts, column, 0, keepdims=False)
    ends = jnp.cumsum(counts)
    starts = ends - counts
    padded = padded_inverse(coarse_inverse, starts, counts)

    own_start = lax.dynamic_index_in_dim(starts, row, 0, keepdims=False)
    own_count = lax.dynamic_index_in_dim(counts, row, 0, keepdims=False)
    base = column * column_width + own_start
    owner = jnp.minimum(base // 32, rows - 2)

    def place(chip):
        return (chip // (ny * nz)) * (ny * nz) + (chip % ny) * nz + (chip // ny) % nz

    info = jnp.stack([place(owner), place(owner + 1), base - 32 * owner, own_count])

    doubled = jnp.stack([row > 0, row < rows - 1, column == 1, column == 0])
    factor = jnp.repeat(jnp.where(doubled, 2.0, 1.0), face)[None, :]

    def precondition(rounded):
        weights = lax.dot_general(
            mode_block, rounded, (((1,), (1,)), ((), ())), preferred_element_type=jnp.float32
        ).astype(jnp.bfloat16)
        inner = (rounded.astype(jnp.float32) * factor).astype(jnp.bfloat16)
        smoothed = jnp.dot(inner, precond_block, preferred_element_type=jnp.float32).astype(
            jnp.bfloat16
        )
        local = jump(smoothed)
        partial = coarse_product(padded, gather_blocks(pack(weights)))
        partner = lax.ppermute(partial, "c", [(0, 1), (1, 0)])
        values = gather_blocks((partial + partner).astype(jnp.bfloat16))
        return local + lift(info, values, mode_block)

    disp = jnp.dot(local_loads, flex_block, preferred_element_type=jnp.float32).astype(jnp.bfloat16)
    residual = jump(disp)
    direction = precondition(residual.astype(jnp.bfloat16))
    energy = None
    multipliers = None
    for step_number in range(ITERS):
        moved = jump(direction.astype(jnp.bfloat16)).astype(jnp.bfloat16)
        image = jump(
            jnp.dot(moved, flex_block, preferred_element_type=jnp.float32).astype(jnp.bfloat16)
        )
        curvature = jnp.sum(direction * image, axis=1)
        if energy is None:
            both = jnp.concatenate([jnp.sum(residual * direction, axis=1), curvature])
            both = total(both[None, :])[0]
            energy, curvature = both[:64], both[64:]
        else:
            curvature = total(curvature[None, :])[0]
        size = (energy / curvature)[:, None]
        multipliers = size * direction if multipliers is None else multipliers + size * direction
        residual = residual - size * image
        if step_number + 1 < ITERS:
            fresh_z = precondition(residual.astype(jnp.bfloat16))
            fresh = total(jnp.sum(residual * fresh_z, axis=1)[None, :])[0]
            direction = fresh_z + (fresh / energy)[:, None] * direction
            energy = fresh
    return (multipliers.astype(jnp.bfloat16)[None, None], residual.astype(jnp.bfloat16)[None, None])


def solution(mesh):
    split = Mesh(mesh.devices.reshape(XYZ + (2,)), WIDE + ("c",))
    blocks = P(WIDE, "c", None, None)
    return jax.shard_map(
        shards,
        mesh=split,
        in_specs=(blocks, blocks, blocks, blocks, P(WIDE, "c"), P()),
        out_specs=(blocks, blocks),
        check_vma=False,
    )
```

```python
import jax
import jax.numpy as jnp
from jax import lax
from jax.experimental import pallas as pl
from jax.experimental.pallas import tpu as pltpu
from jax.sharding import Mesh, PartitionSpec as P

XYZ = (4, 16, 4)
WIDE = ("x", "z", "y")
INTERPRET = False


def spread(values, axes):
    count = lax.axis_size(axes)
    copies = jnp.broadcast_to(values[None], (count,) + values.shape)
    return lax.all_to_all(copies, axes, 0, 0, tiled=False)


def gather_blocks(block):
    stage = spread(block, "z")
    stage = spread(stage, ("x", "y"))
    return stage.reshape((-1,) + block.shape)


def total(partial):
    stage = jnp.sum(spread(partial, ("x", "y", "c")), axis=0)
    return jnp.sum(spread(stage, "z"), axis=0)


def neighbours(values):
    load_count, width = values.shape
    face = width // 4
    rows = lax.axis_size(WIDE)
    column = lax.axis_index("c")
    down = [(i, i + 1) for i in range(rows - 1)]
    up = [(i + 1, i) for i in range(rows - 1)]
    north, south, west, east = (values[:, k * face : (k + 1) * face] for k in range(4))
    from_above = lax.ppermute(south, WIDE, down)
    from_below = lax.ppermute(north, WIDE, up)
    side = lax.ppermute(jnp.where(column == 0, east, west), "c", [(0, 1), (1, 0)])
    nothing = jnp.zeros_like(side)
    from_west = jnp.where(column == 1, side, nothing)
    from_east = jnp.where(column == 0, side, nothing)
    return jnp.concatenate([from_above, from_below, from_west, from_east], axis=1)


def jump(values):
    return values.astype(jnp.float32) - neighbours(values).astype(jnp.float32)


def pack(wide_rows):
    half = wide_rows.shape[0] // 2
    return jnp.concatenate([wide_rows[:half], wide_rows[half:]], axis=1)


def pad_kernel(first_ref, source_ref, block_ref, out_ref):
    rows, columns = block_ref.shape
    window = min(384, columns)
    chunks = out_ref.shape[1] // 128
    position = lax.broadcasted_iota(jnp.int32, (window, 128), 0)
    own_row = lax.broadcasted_iota(jnp.int32, (rows, window), 0) + first_ref[chunks]
    own_column = lax.broadcasted_iota(jnp.int32, (rows, window), 1)

    def step(chunk, carry):
        low = pl.multiple_of(first_ref[chunk] * 128, 128)
        unit = jnp.where(own_column + low == own_row, 1.0, 0.0).astype(jnp.bfloat16)
        part = jnp.concatenate([block_ref[:, pl.ds(low, window)], unit], axis=0)
        target = pl.multiple_of(chunk * 128, 128)
        for half in range(2):
            hot = jnp.where(position == source_ref[half, chunk] - low, 1.0, 0.0).astype(jnp.bfloat16)
            chosen = jnp.dot(part, hot, preferred_element_type=jnp.float32)
            out_ref[2 * half * rows : 2 * (half + 1) * rows, pl.ds(target, 128)] = chosen.astype(
                jnp.bfloat16
            )
        return carry

    lax.fori_loop(0, chunks, step, 0)


def padded_inverse(block, starts, counts, own_first):
    rows, columns = block.shape
    subdomains = counts.shape[0]
    slots = 32
    half_slots = slots // 2
    rank = jnp.arange(slots, dtype=jnp.int32)
    source = jnp.where(rank[None, :] < counts[:, None], starts[:, None] + rank[None, :], -1)
    chunks = subdomains * half_slots // 128
    source = source.reshape(subdomains, 2, half_slots).transpose(1, 0, 2).reshape(2, chunks, 1, 128)
    window = min(384, columns)
    first = jnp.minimum(starts.reshape(chunks, -1)[:, 0] // 128, (columns - window) // 128)
    first = jnp.concatenate([first, own_first[None]])
    return pl.pallas_call(
        pad_kernel,
        out_shape=jax.ShapeDtypeStruct((4 * rows, subdomains * half_slots), jnp.bfloat16),
        in_specs=[
            pl.BlockSpec(memory_space=pltpu.SMEM),
            pl.BlockSpec(memory_space=pltpu.VMEM),
            pl.BlockSpec(memory_space=pltpu.VMEM),
        ],
        out_specs=pl.BlockSpec(memory_space=pltpu.VMEM),
        interpret=INTERPRET,
        name="pad_inverse",
    )(first, source, block)


def product_kernel(padded_ref, blocks_ref, out_ref):
    nx, nz, ny = XYZ
    rows = padded_ref.shape[0] // 4
    half = rows // 2
    length = nz * ny * half
    result = jnp.zeros((4 * rows, 128), jnp.float32)
    for x in range(nx):
        order = [x * ny * nz + y * nz + z for z in range(nz) for y in range(ny)]
        part = jnp.concatenate([blocks_ref[p, 0:half, :] for p in order], axis=0)
        result += jnp.dot(
            padded_ref[:, x * length : (x + 1) * length], part, preferred_element_type=jnp.float32
        )
    joined = result[: 2 * rows] + pltpu.roll(result[2 * rows :], 64, 1)
    lane = lax.broadcasted_iota(jnp.int32, (half, 128), 1)
    for k in range(2):
        low = joined[2 * k * half : (2 * k + 1) * half]
        high = joined[(2 * k + 1) * half : (2 * k + 2) * half]
        out_ref[k * half : (k + 1) * half, :] = jnp.where(lane < 64, low, pltpu.roll(high, 64, 1))
    if out_ref.shape[0] > rows:
        sums = jnp.zeros((8, 128), jnp.float32)
        for p in range(blocks_ref.shape[0]):
            sums += blocks_ref[p, half : half + 8, :].astype(jnp.float32)
        out_ref[rows : rows + 8, :] = sums


def coarse_product(padded, blocks):
    rows = padded.shape[0] // 4
    return pl.pallas_call(
        product_kernel,
        out_shape=jax.ShapeDtypeStruct((rows + blocks.shape[1] - rows // 2, 128), jnp.float32),
        interpret=INTERPRET,
        name="coarse_product",
    )(padded, blocks)


def in_pieces(values):
    rest = values
    pieces = []
    for _ in range(3):
        piece = lax.reduce_precision(rest, 8, 7)
        pieces.append(piece)
        rest = rest - piece
    pieces.append(jnp.zeros((8 - len(pieces), values.shape[1]), jnp.float32))
    return jnp.concatenate(pieces, axis=0).astype(jnp.bfloat16)


def swapped_sum(partial):
    return partial + lax.ppermute(partial, "c", [(0, 1), (1, 0)])


def lift_kernel(info_ref, low_ref, high_ref, modes_ref, out_ref):
    slots = modes_ref.shape[0]
    half_slots = slots // 2
    window = jnp.concatenate([low_ref[0, 0:half_slots, :], high_ref[0, 0:half_slots, :]], axis=0)
    rank = lax.broadcasted_iota(jnp.int32, (slots, slots), 0)
    column = lax.broadcasted_iota(jnp.int32, (slots, slots), 1)
    offset = info_ref[2] + rank
    row = (offset // 32) * 16 + offset % 16
    half = (offset // 16) % 2
    hit = jnp.logical_and(row == column, rank < info_ref[3])
    first = jnp.where(jnp.logical_and(hit, half == 0), 1.0, 0.0).astype(jnp.bfloat16)
    second = jnp.where(jnp.logical_and(hit, half == 1), 1.0, 0.0).astype(jnp.bfloat16)
    picked = jnp.dot(first, window, preferred_element_type=jnp.float32) + pltpu.roll(
        jnp.dot(second, window, preferred_element_type=jnp.float32), 64, 1
    )
    lifted = lax.dot_general(
        picked.astype(jnp.bfloat16),
        modes_ref[...],
        (((0,), (0,)), ((), ())),
        preferred_element_type=jnp.float32,
    )
    out_ref[...] = lifted[: out_ref.shape[0]]


def lift(info, blocks, modes):
    block_rows = blocks.shape[1]
    load_count = 64
    width = modes.shape[1]
    return pl.pallas_call(
        lift_kernel,
        out_shape=jax.ShapeDtypeStruct((load_count, width), jnp.float32),
        grid_spec=pltpu.PrefetchScalarGridSpec(
            num_scalar_prefetch=1,
            grid=(1,),
            in_specs=[
                pl.BlockSpec((1, block_rows, 128), lambda i, info: (info[0], 0, 0)),
                pl.BlockSpec((1, block_rows, 128), lambda i, info: (info[1], 0, 0)),
                pl.BlockSpec(modes.shape, lambda i, info: (0, 0)),
            ],
            out_specs=pl.BlockSpec((load_count, width), lambda i, info: (0, 0)),
        ),
        interpret=INTERPRET,
        name="lift",
    )(info, blocks, blocks, modes)


def shards(loads, flexibility, dirichlet, modes, coarse_inverse, mode_counts):
    local_loads = loads[0, 0]
    flex_block = flexibility[0, 0]
    precond_block = dirichlet[0, 0]
    mode_block = modes[0, 0]
    nx, nz, ny = XYZ
    rows = lax.axis_size(WIDE)
    row = lax.axis_index(WIDE)
    column = lax.axis_index("c")
    column_width = coarse_inverse.shape[1]
    face = local_loads.shape[1] // 4

    counts = lax.dynamic_index_in_dim(mode_counts, column, 0, keepdims=False)
    ends = jnp.cumsum(counts)
    starts = ends - counts
    padded = padded_inverse(coarse_inverse, starts, counts, 32 * row - column * column_width)

    own_start = lax.dynamic_index_in_dim(starts, row, 0, keepdims=False)
    own_count = lax.dynamic_index_in_dim(counts, row, 0, keepdims=False)
    base = column * column_width + own_start
    owner = jnp.minimum(base // 32, rows - 2)

    def place(chip):
        return (chip // (ny * nz)) * (ny * nz) + (chip % ny) * nz + (chip // ny) % nz

    info = jnp.stack([place(owner), place(owner + 1), base - 32 * owner, own_count])

    doubled = jnp.stack([row > 0, row < rows - 1, column == 1, column == 0])
    factor = jnp.repeat(jnp.where(doubled, 2.0, 1.0), face)[None, :]

    def weigh(rounded):
        return lax.dot_general(
            mode_block, rounded, (((1,), (1,)), ((), ())), preferred_element_type=jnp.float32
        )

    def smooth(rounded):
        inner = (rounded.astype(jnp.float32) * factor).astype(jnp.bfloat16)
        return jnp.dot(inner, precond_block, preferred_element_type=jnp.float32).astype(
            jnp.bfloat16
        )

    def apply_flex(values):
        return jnp.dot(values, flex_block, preferred_element_type=jnp.float32).astype(jnp.bfloat16)

    def operator_input(direction):
        return jump(direction.astype(jnp.bfloat16)).astype(jnp.bfloat16)

    def load_dot(left, right):
        return jnp.sum(left.astype(jnp.float32) * right.astype(jnp.float32), axis=1)

    residual = jump(apply_flex(local_loads))
    rounded = residual.astype(jnp.bfloat16)
    smoothed = smooth(rounded)
    first_sums = swapped_sum(
        coarse_product(padded, gather_blocks(pack(weigh(rounded).astype(jnp.bfloat16))))
    )
    half_slots = first_sums.shape[0] // 2
    values = gather_blocks(first_sums[:half_slots].astype(jnp.bfloat16))
    direction = jump(smoothed) + lift(info, values, mode_block)

    moved = operator_input(direction)
    pushed = apply_flex(moved)
    partials = jnp.concatenate([load_dot(residual, direction), load_dot(moved, pushed)])[None, :]
    image = jump(pushed)
    image_high = lax.reduce_precision(image, 8, 7)
    image_low = (image - image_high).astype(jnp.bfloat16)
    image_weights = weigh(image_high.astype(jnp.bfloat16)) + weigh(image_low)
    block = jnp.concatenate([pack(image_weights.astype(jnp.bfloat16)), in_pieces(partials)], axis=0)
    second_sums = swapped_sum(coarse_product(padded, gather_blocks(block)))
    totals = jnp.sum(second_sums[2 * half_slots :], axis=0)
    energy = totals[:64]
    size = energy / totals[64:]
    multipliers = size[:, None] * direction
    residual = residual - size[:, None] * image

    packed = first_sums - jnp.tile(size, 2)[None, :] * second_sums[: 2 * half_slots]
    rounded = residual.astype(jnp.bfloat16)
    smoothed = smooth(rounded)
    coarse_values = lax.reduce_precision(packed[:half_slots], 8, 7)
    coarse_energy = jnp.sum(coarse_values * packed[half_slots:], axis=0)
    local_energy = load_dot(residual * factor, smoothed)
    partial = local_energy + 0.5 * (coarse_energy[:64] + coarse_energy[64:])
    partial = jnp.concatenate([partial, jnp.zeros_like(partial)])[None, :]
    block = jnp.concatenate([coarse_values.astype(jnp.bfloat16), in_pieces(partial)], axis=0)
    values = gather_blocks(block)
    sums = jnp.sum(values[:, half_slots:, :].astype(jnp.float32), axis=(0, 1))[None, :]
    fresh = swapped_sum(sums)[0, :64]
    direction = (
        jump(smoothed)
        + lift(info, values, mode_block)
        + (fresh / energy)[:, None] * direction
    )

    moved = operator_input(direction)
    pushed = apply_flex(moved)
    curvature = total(load_dot(moved, pushed)[None, :])[0]
    image = jump(pushed)
    size = (fresh / curvature)[:, None]
    multipliers = multipliers + size * direction
    residual = residual - size * image
    return (multipliers.astype(jnp.bfloat16)[None, None], residual.astype(jnp.bfloat16)[None, None])


def solution(mesh):
    split = Mesh(mesh.devices.reshape(XYZ + (2,)), WIDE + ("c",))
    blocks = P(WIDE, "c", None, None)
    return jax.shard_map(
        shards,
        mesh=split,
        in_specs=(blocks, blocks, blocks, blocks, P(WIDE, "c"), P()),
        out_specs=(blocks, blocks),
        check_vma=False,
    )
```

```python
import jax
import jax.numpy as jnp
from jax import lax
from jax.experimental import pallas as pl
from jax.experimental.pallas import tpu as pltpu
from jax.sharding import Mesh, PartitionSpec as P

XYZ = (4, 16, 4)
WIDE = ("x", "z", "y")
INTERPRET = False


def spread(values, axes):
    count = lax.axis_size(axes)
    copies = jnp.broadcast_to(values[None], (count,) + values.shape)
    return lax.all_to_all(copies, axes, 0, 0, tiled=False)


def along_z(block):
    return spread(block, "z").reshape(-1, block.shape[1])


def across(block):
    return spread(block, ("x", "y"))


def gather_with_sum(block, partial):
    rows = block.shape[0]
    stage = spread(jnp.concatenate([block, in_pieces(partial)], axis=0), "z")
    sums = jnp.sum(stage[:, rows:, :].astype(jnp.float32), axis=(0, 1))[None, :]
    rest = stage[:, :rows, :].reshape(-1, block.shape[1])
    return across(jnp.concatenate([rest, in_pieces(sums)], axis=0))


def total(partial):
    stage = jnp.sum(spread(partial, ("x", "y", "c")), axis=0)
    return jnp.sum(spread(stage, "z"), axis=0)


def neighbours(values):
    load_count, width = values.shape
    face = width // 4
    rows = lax.axis_size(WIDE)
    column = lax.axis_index("c")
    down = [(i, i + 1) for i in range(rows - 1)]
    up = [(i + 1, i) for i in range(rows - 1)]
    north, south, west, east = (values[:, k * face : (k + 1) * face] for k in range(4))
    from_above = lax.ppermute(south, WIDE, down)
    from_below = lax.ppermute(north, WIDE, up)
    side = lax.ppermute(jnp.where(column == 0, east, west), "c", [(0, 1), (1, 0)])
    nothing = jnp.zeros_like(side)
    from_west = jnp.where(column == 1, side, nothing)
    from_east = jnp.where(column == 0, side, nothing)
    return jnp.concatenate([from_above, from_below, from_west, from_east], axis=1)


def jump(values):
    return values.astype(jnp.float32) - neighbours(values).astype(jnp.float32)


def pack(wide_rows):
    half = wide_rows.shape[0] // 2
    return jnp.concatenate([wide_rows[:half], wide_rows[half:]], axis=1)


def pad_kernel(first_ref, source_ref, block_ref, out_ref):
    rows, columns = block_ref.shape
    window = min(384, columns)
    chunks = out_ref.shape[1] // 128
    position = lax.broadcasted_iota(jnp.int32, (window, 128), 0)
    own_row = lax.broadcasted_iota(jnp.int32, (rows, window), 0) + first_ref[chunks]
    own_column = lax.broadcasted_iota(jnp.int32, (rows, window), 1)

    def step(chunk, carry):
        low = pl.multiple_of(first_ref[chunk] * 128, 128)
        unit = jnp.where(own_column + low == own_row, 1.0, 0.0).astype(jnp.bfloat16)
        part = jnp.concatenate([block_ref[:, pl.ds(low, window)], unit], axis=0)
        target = pl.multiple_of(chunk * 128, 128)
        for half in range(2):
            hot = jnp.where(position == source_ref[half, chunk] - low, 1.0, 0.0).astype(jnp.bfloat16)
            chosen = jnp.dot(part, hot, preferred_element_type=jnp.float32)
            out_ref[2 * half * rows : 2 * (half + 1) * rows, pl.ds(target, 128)] = chosen.astype(
                jnp.bfloat16
            )
        return carry

    lax.fori_loop(0, chunks, step, 0)


def padded_inverse(block, starts, counts, own_first):
    rows, columns = block.shape
    subdomains = counts.shape[0]
    slots = 32
    half_slots = slots // 2
    rank = jnp.arange(slots, dtype=jnp.int32)
    source = jnp.where(rank[None, :] < counts[:, None], starts[:, None] + rank[None, :], -1)
    chunks = subdomains * half_slots // 128
    source = source.reshape(subdomains, 2, half_slots).transpose(1, 0, 2).reshape(2, chunks, 1, 128)
    window = min(384, columns)
    first = jnp.minimum(starts.reshape(chunks, -1)[:, 0] // 128, (columns - window) // 128)
    first = jnp.concatenate([first, own_first[None]])
    return pl.pallas_call(
        pad_kernel,
        out_shape=jax.ShapeDtypeStruct((4 * rows, subdomains * half_slots), jnp.bfloat16),
        in_specs=[
            pl.BlockSpec(memory_space=pltpu.SMEM),
            pl.BlockSpec(memory_space=pltpu.VMEM),
            pl.BlockSpec(memory_space=pltpu.VMEM),
        ],
        out_specs=pl.BlockSpec(memory_space=pltpu.VMEM),
        interpret=INTERPRET,
        name="pad_inverse",
    )(first, source, block)


def product_kernel(padded_ref, blocks_ref, out_ref):
    nx, nz, ny = XYZ
    rows = padded_ref.shape[0] // 4
    half = rows // 2
    length = nz * ny * half
    result = jnp.zeros((4 * rows, 128), jnp.float32)
    for x in range(nx):
        order = [(x * ny + y, z * half) for z in range(nz) for y in range(ny)]
        part = jnp.concatenate([blocks_ref[p, r : r + half, :] for p, r in order], axis=0)
        result += jnp.dot(
            padded_ref[:, x * length : (x + 1) * length], part, preferred_element_type=jnp.float32
        )
    joined = result[: 2 * rows] + pltpu.roll(result[2 * rows :], 64, 1)
    lane = lax.broadcasted_iota(jnp.int32, (half, 128), 1)
    for k in range(2):
        low = joined[2 * k * half : (2 * k + 1) * half]
        high = joined[(2 * k + 1) * half : (2 * k + 2) * half]
        out_ref[k * half : (k + 1) * half, :] = jnp.where(lane < 64, low, pltpu.roll(high, 64, 1))
    if out_ref.shape[0] > rows:
        sums = jnp.zeros((8, 128), jnp.float32)
        for p in range(blocks_ref.shape[0]):
            sums += blocks_ref[p, nz * half : nz * half + 8, :].astype(jnp.float32)
        out_ref[rows : rows + 8, :] = sums


def coarse_product(padded, blocks):
    rows = padded.shape[0] // 4
    return pl.pallas_call(
        product_kernel,
        out_shape=jax.ShapeDtypeStruct((rows + blocks.shape[1] - XYZ[1] * (rows // 2), 128), jnp.float32),
        interpret=INTERPRET,
        name="coarse_product",
    )(padded, blocks)


def in_pieces(values):
    rest = values
    pieces = []
    for _ in range(3):
        piece = lax.reduce_precision(rest, 8, 7)
        pieces.append(piece)
        rest = rest - piece
    pieces.append(jnp.zeros((8 - len(pieces), values.shape[1]), jnp.float32))
    return jnp.concatenate(pieces, axis=0).astype(jnp.bfloat16)


def swapped_sum(partial):
    return partial + lax.ppermute(partial, "c", [(0, 1), (1, 0)])


def direction_kernel(info_ref, *refs):
    blocks = refs[:8]
    modes_ref, near_modes_ref, smoothed_ref, near_smoothed_ref, exists_ref = refs[8:13]
    out_ref, near_ref, moved_ref = refs[-3:]
    slots, width = modes_ref.shape
    load_count = out_ref.shape[0]
    face = width // 4
    half_slots = slots // 2
    rank = lax.broadcasted_iota(jnp.int32, (slots, slots), 0)
    column = lax.broadcasted_iota(jnp.int32, (slots, slots), 1)

    def lifted(which, rows):
        window = jnp.concatenate([blocks[2 * which][0], blocks[2 * which + 1][0]], axis=0)
        offset = info_ref[4 * which + 2] + rank
        row = (offset // slots) * half_slots + offset % half_slots
        second = (offset // half_slots) % 2 == 1
        hit = jnp.logical_and(row == column, rank < info_ref[4 * which + 3])
        low = jnp.where(jnp.logical_and(hit, jnp.logical_not(second)), 1.0, 0.0)
        high = jnp.where(jnp.logical_and(hit, second), 1.0, 0.0)
        picked = jnp.dot(
            low.astype(jnp.bfloat16), window, preferred_element_type=jnp.float32
        ) + pltpu.roll(
            jnp.dot(high.astype(jnp.bfloat16), window, preferred_element_type=jnp.float32), 64, 1
        )
        result = lax.dot_general(
            picked.astype(jnp.bfloat16),
            rows,
            (((0,), (0,)), ((), ())),
            preferred_element_type=jnp.float32,
        )
        return result[:load_count]

    local = smoothed_ref[...].astype(jnp.float32) - near_smoothed_ref[...].astype(jnp.float32)
    direction = local + lifted(0, modes_ref[...])
    near_lifted = jnp.concatenate(
        [
            lifted(1, near_modes_ref[:, :face]),
            lifted(2, near_modes_ref[:, face : 2 * face]),
            lifted(3, near_modes_ref[:, 2 * face :]),
        ],
        axis=1,
    )
    near = near_lifted - exists_ref[...] * local
    if len(refs) > 16:
        ratio_ref, previous_ref, near_previous_ref = refs[13:16]
        ratio = ratio_ref[...]
        direction += ratio * previous_ref[...]
        near += ratio * near_previous_ref[...]
    out_ref[...] = direction
    near_ref[...] = near
    moved_ref[...] = (
        direction.astype(jnp.bfloat16).astype(jnp.float32)
        - near.astype(jnp.bfloat16).astype(jnp.float32)
    ).astype(jnp.bfloat16)


def next_direction(info, blocks, modes, near_modes, smoothed, near_smoothed, exists, *previous):
    half_slots = modes.shape[0] // 2
    nz = XYZ[1]

    def block_spec(k):
        return pl.BlockSpec(
            (1, half_slots, 128), lambda i, info: (info[k] // nz, info[k] % nz, 0)
        )

    def whole(array):
        return pl.BlockSpec(array.shape, lambda i, info: (0, 0))

    rest = (modes, near_modes, smoothed, near_smoothed, exists) + previous
    shape = smoothed.shape
    return pl.pallas_call(
        direction_kernel,
        out_shape=(
            jax.ShapeDtypeStruct(shape, jnp.float32),
            jax.ShapeDtypeStruct(shape, jnp.float32),
            jax.ShapeDtypeStruct(shape, jnp.bfloat16),
        ),
        grid_spec=pltpu.PrefetchScalarGridSpec(
            num_scalar_prefetch=1,
            grid=(1,),
            in_specs=[block_spec(4 * (k // 2) + k % 2) for k in range(8)] + [whole(r) for r in rest],
            out_specs=(whole(smoothed), whole(smoothed), whole(smoothed)),
        ),
        interpret=INTERPRET,
        name="next_direction",
    )(info, *([blocks] * 8), *rest)


def shards(loads, flexibility, dirichlet, modes, coarse_inverse, mode_counts):
    local_loads = loads[0, 0]
    flex_block = flexibility[0, 0]
    precond_block = dirichlet[0, 0]
    mode_block = modes[0, 0]
    nx, nz, ny = XYZ
    rows = lax.axis_size(WIDE)
    row = lax.axis_index(WIDE)
    column = lax.axis_index("c")
    column_width = coarse_inverse.shape[1]
    face = local_loads.shape[1] // 4

    all_ends = jnp.cumsum(mode_counts, axis=1)
    all_starts = all_ends - mode_counts
    own_first = column == 0
    counts = jnp.where(own_first, mode_counts[0], mode_counts[1])
    starts = jnp.where(own_first, all_starts[0], all_starts[1])
    padded = padded_inverse(coarse_inverse, starts, counts, 32 * row - column * column_width)

    column_of = jnp.stack([column, column, column, 1 - column])
    row_of = jnp.stack([row, row - 1, row + 1, row])
    chosen = jnp.logical_and(
        jnp.arange(rows)[None, None, :] == row_of[:, None, None],
        jnp.arange(2)[None, :, None] == column_of[:, None, None],
    )
    start_of = jnp.sum(jnp.where(chosen, all_starts[None], 0), axis=(1, 2))
    count_of = jnp.sum(jnp.where(chosen, mode_counts[None], 0), axis=(1, 2))
    base = column_of * column_width + start_of
    owner = jnp.minimum(base // 32, rows - 2)

    def place(chip):
        return (chip // (ny * nz)) * (ny * nz) + (chip % ny) * nz + (chip // ny) % nz

    info = jnp.stack([place(owner), place(owner + 1), base - 32 * owner, count_of], axis=1)
    info = info.reshape(-1).astype(jnp.int32)

    has_neighbour = jnp.stack([row > 0, row < rows - 1, column == 1, column == 0])
    exists = jnp.repeat(jnp.where(has_neighbour, 1.0, 0.0), face)[None, :]
    factor = 1.0 + exists
    near_modes = neighbours(mode_block)

    def weigh(rounded):
        return lax.dot_general(
            mode_block, rounded, (((1,), (1,)), ((), ())), preferred_element_type=jnp.float32
        )

    def smooth(rounded):
        inner = (rounded.astype(jnp.float32) * factor).astype(jnp.bfloat16)
        return jnp.dot(inner, precond_block, preferred_element_type=jnp.float32).astype(
            jnp.bfloat16
        )

    def apply_flex(values):
        return jnp.dot(values, flex_block, preferred_element_type=jnp.float32).astype(jnp.bfloat16)

    def load_dot(left, right):
        return jnp.sum(left.astype(jnp.float32) * right.astype(jnp.float32), axis=1)

    residual = jump(apply_flex(local_loads))
    rounded = residual.astype(jnp.bfloat16)
    smoothed = smooth(rounded)
    near_smoothed = neighbours(smoothed)
    stage = along_z(pack(weigh(rounded).astype(jnp.bfloat16)))
    stage, padded, info, near_modes, near_smoothed = lax.optimization_barrier(
        (stage, padded, info, near_modes, near_smoothed)
    )
    first_sums = swapped_sum(coarse_product(padded, across(stage)))
    half_slots = first_sums.shape[0] // 2
    values = across(along_z(first_sums[:half_slots].astype(jnp.bfloat16)))
    direction, near_direction, moved = next_direction(
        info, values, mode_block, near_modes, smoothed, near_smoothed, exists
    )

    pushed = apply_flex(moved)
    partials = jnp.concatenate([load_dot(residual, direction), load_dot(moved, pushed)])[None, :]
    image = jump(pushed)
    image_high = lax.reduce_precision(image, 8, 7)
    image_low = (image - image_high).astype(jnp.bfloat16)
    image_weights = weigh(image_high.astype(jnp.bfloat16)) + weigh(image_low)
    blocks = gather_with_sum(pack(image_weights.astype(jnp.bfloat16)), partials)
    second_sums = swapped_sum(coarse_product(padded, blocks))
    totals = jnp.sum(second_sums[2 * half_slots :], axis=0)
    energy = totals[:64]
    size = energy / totals[64:]
    multipliers = size[:, None] * direction
    residual = residual - size[:, None] * image

    packed = first_sums - jnp.tile(size, 2)[None, :] * second_sums[: 2 * half_slots]
    rounded = residual.astype(jnp.bfloat16)
    smoothed = smooth(rounded)
    coarse_values = lax.reduce_precision(packed[:half_slots], 8, 7)
    coarse_energy = jnp.sum(coarse_values * packed[half_slots:], axis=0)
    local_energy = load_dot(residual * factor, smoothed)
    partial = local_energy + 0.5 * (coarse_energy[:64] + coarse_energy[64:])
    partial = jnp.concatenate([partial, jnp.zeros_like(partial)])[None, :]
    near_smoothed = neighbours(smoothed)
    values = gather_with_sum(coarse_values.astype(jnp.bfloat16), partial)
    sums = jnp.sum(values[:, nz * half_slots :, :].astype(jnp.float32), axis=(0, 1))[None, :]
    fresh = swapped_sum(sums)[0, :64]
    direction, near_direction, moved = next_direction(
        info,
        values,
        mode_block,
        near_modes,
        smoothed,
        near_smoothed,
        exists,
        (fresh / energy)[:, None],
        direction,
        near_direction,
    )

    pushed = apply_flex(moved)
    curvature = total(load_dot(moved, pushed)[None, :])[0]
    image = jump(pushed)
    size = (fresh / curvature)[:, None]
    multipliers = multipliers + size * direction
    residual = residual - size * image
    return (multipliers.astype(jnp.bfloat16)[None, None], residual.astype(jnp.bfloat16)[None, None])


def solution(mesh):
    split = Mesh(mesh.devices.reshape(XYZ + (2,)), WIDE + ("c",))
    blocks = P(WIDE, "c", None, None)
    return jax.shard_map(
        shards,
        mesh=split,
        in_specs=(blocks, blocks, blocks, blocks, P(WIDE, "c"), P()),
        out_specs=(blocks, blocks),
        check_vma=False,
    )
```

```python
import jax
import jax.numpy as jnp
from jax import lax
from jax.experimental import pallas as pl
from jax.experimental.pallas import tpu as pltpu
from jax.sharding import Mesh, PartitionSpec as P

XYZ = (4, 16, 4)
WIDE = ("x", "z", "y")
INTERPRET = False


def spread(values, axes):
    count = lax.axis_size(axes)
    copies = jnp.broadcast_to(values[None], (count,) + values.shape)
    return lax.all_to_all(copies, axes, 0, 0, tiled=False)


def along_z(block):
    return spread(block, "z").reshape(-1, block.shape[1])


def across(block):
    return spread(block, ("x", "y"))


def gather_with_sum(block, partial):
    rows = block.shape[0]
    stage = spread(jnp.concatenate([block, in_pieces(partial)], axis=0), "z")
    sums = jnp.sum(stage[:, rows:, :].astype(jnp.float32), axis=(0, 1))[None, :]
    rest = stage[:, :rows, :].reshape(-1, block.shape[1])
    return across(jnp.concatenate([rest, in_pieces(sums)], axis=0))


def total(partial):
    stage = jnp.sum(spread(partial, ("x", "y", "c")), axis=0)
    return jnp.sum(spread(stage, "z"), axis=0)


def neighbours(values):
    load_count, width = values.shape
    face = width // 4
    rows = lax.axis_size(WIDE)
    column = lax.axis_index("c")
    down = [(i, i + 1) for i in range(rows - 1)]
    up = [(i + 1, i) for i in range(rows - 1)]
    north, south, west, east = (values[:, k * face : (k + 1) * face] for k in range(4))
    from_above = lax.ppermute(south, WIDE, down)
    from_below = lax.ppermute(north, WIDE, up)
    side = lax.ppermute(jnp.where(column == 0, east, west), "c", [(0, 1), (1, 0)])
    nothing = jnp.zeros_like(side)
    from_west = jnp.where(column == 1, side, nothing)
    from_east = jnp.where(column == 0, side, nothing)
    return jnp.concatenate([from_above, from_below, from_west, from_east], axis=1)


def jump(values):
    return values.astype(jnp.float32) - neighbours(values).astype(jnp.float32)


def pack(wide_rows):
    half = wide_rows.shape[0] // 2
    return jnp.concatenate([wide_rows[:half], wide_rows[half:]], axis=1)


def pad_kernel(first_ref, source_ref, block_ref, out_ref):
    rows, columns = block_ref.shape
    window = min(384, columns)
    chunks = out_ref.shape[1] // 128
    position = lax.broadcasted_iota(jnp.int32, (window, 128), 0)
    own_row = lax.broadcasted_iota(jnp.int32, (rows, window), 0) + first_ref[chunks]
    own_column = lax.broadcasted_iota(jnp.int32, (rows, window), 1)

    def step(chunk, carry):
        low = pl.multiple_of(first_ref[chunk] * 128, 128)
        unit = jnp.where(own_column + low == own_row, 1.0, 0.0).astype(jnp.bfloat16)
        part = jnp.concatenate([block_ref[:, pl.ds(low, window)], unit], axis=0)
        target = pl.multiple_of(chunk * 128, 128)
        for half in range(2):
            hot = jnp.where(position == source_ref[half, chunk] - low, 1.0, 0.0).astype(jnp.bfloat16)
            chosen = jnp.dot(part, hot, preferred_element_type=jnp.float32)
            out_ref[2 * half * rows : 2 * (half + 1) * rows, pl.ds(target, 128)] = chosen.astype(
                jnp.bfloat16
            )
        return carry

    lax.fori_loop(0, chunks, step, 0)


def padded_inverse(block, starts, counts, own_first):
    rows, columns = block.shape
    subdomains = counts.shape[0]
    slots = 32
    half_slots = slots // 2
    rank = jnp.arange(slots, dtype=jnp.int32)
    source = jnp.where(rank[None, :] < counts[:, None], starts[:, None] + rank[None, :], -1)
    chunks = subdomains * half_slots // 128
    source = source.reshape(subdomains, 2, half_slots).transpose(1, 0, 2).reshape(2, chunks, 1, 128)
    window = min(384, columns)
    first = jnp.minimum(starts.reshape(chunks, -1)[:, 0] // 128, (columns - window) // 128)
    first = jnp.concatenate([first, own_first[None]])
    return pl.pallas_call(
        pad_kernel,
        out_shape=jax.ShapeDtypeStruct((4 * rows, subdomains * half_slots), jnp.bfloat16),
        in_specs=[
            pl.BlockSpec(memory_space=pltpu.SMEM),
            pl.BlockSpec(memory_space=pltpu.VMEM),
            pl.BlockSpec(memory_space=pltpu.VMEM),
        ],
        out_specs=pl.BlockSpec(memory_space=pltpu.VMEM),
        interpret=INTERPRET,
        compiler_params=pltpu.CompilerParams(vmem_limit_bytes=8 << 20),
        name="pad_inverse",
    )(first, source, block)


def product_kernel(padded_ref, blocks_ref, out_ref):
    nx, nz, ny = XYZ
    rows = padded_ref.shape[0] // 4
    half = rows // 2
    length = nz * ny * half
    result = jnp.zeros((4 * rows, 128), jnp.float32)
    for x in range(nx):
        order = [(x * ny + y, z * half) for z in range(nz) for y in range(ny)]
        part = jnp.concatenate([blocks_ref[p, r : r + half, :] for p, r in order], axis=0)
        result += jnp.dot(
            padded_ref[:, x * length : (x + 1) * length], part, preferred_element_type=jnp.float32
        )
    joined = result[: 2 * rows] + pltpu.roll(result[2 * rows :], 64, 1)
    lane = lax.broadcasted_iota(jnp.int32, (half, 128), 1)
    for k in range(2):
        low = joined[2 * k * half : (2 * k + 1) * half]
        high = joined[(2 * k + 1) * half : (2 * k + 2) * half]
        out_ref[k * half : (k + 1) * half, :] = jnp.where(lane < 64, low, pltpu.roll(high, 64, 1))
    if out_ref.shape[0] > rows:
        sums = jnp.zeros((8, 128), jnp.float32)
        for p in range(blocks_ref.shape[0]):
            sums += blocks_ref[p, nz * half : nz * half + 8, :].astype(jnp.float32)
        out_ref[rows : rows + 8, :] = sums


def coarse_product(padded, blocks):
    rows = padded.shape[0] // 4
    return pl.pallas_call(
        product_kernel,
        out_shape=jax.ShapeDtypeStruct((rows + blocks.shape[1] - XYZ[1] * (rows // 2), 128), jnp.float32),
        in_specs=[pl.BlockSpec(memory_space=pltpu.VMEM)] * 2,
        out_specs=pl.BlockSpec(memory_space=pltpu.VMEM),
        interpret=INTERPRET,
        compiler_params=pltpu.CompilerParams(vmem_limit_bytes=8 << 20),
        name="coarse_product",
    )(padded, blocks)


def in_pieces(values):
    rest = values
    pieces = []
    for _ in range(3):
        piece = lax.reduce_precision(rest, 8, 7)
        pieces.append(piece)
        rest = rest - piece
    pieces.append(jnp.zeros((8 - len(pieces), values.shape[1]), jnp.float32))
    return jnp.concatenate(pieces, axis=0).astype(jnp.bfloat16)


def swapped_sum(partial):
    return partial + lax.ppermute(partial, "c", [(0, 1), (1, 0)])


def direction_kernel(info_ref, blocks_ref, *refs):
    modes_ref, near_modes_ref, smoothed_ref, near_smoothed_ref, exists_ref = refs[:5]
    out_ref, near_ref, moved_ref = refs[-3:]
    slots, width = modes_ref.shape
    load_count = out_ref.shape[0]
    face = width // 4
    half_slots = slots // 2
    rank = lax.broadcasted_iota(jnp.int32, (slots, slots), 0)
    column = lax.broadcasted_iota(jnp.int32, (slots, slots), 1)

    def chip_block(chip):
        start = pl.multiple_of((chip % XYZ[1]) * half_slots, half_slots)
        return blocks_ref[chip // XYZ[1], pl.ds(start, half_slots), :]

    def lifted(which, rows):
        window = jnp.concatenate(
            [chip_block(info_ref[4 * which]), chip_block(info_ref[4 * which + 1])], axis=0
        )
        offset = info_ref[4 * which + 2] + rank
        row = (offset // slots) * half_slots + offset % half_slots
        second = (offset // half_slots) % 2 == 1
        hit = jnp.logical_and(row == column, rank < info_ref[4 * which + 3])
        low = jnp.where(jnp.logical_and(hit, jnp.logical_not(second)), 1.0, 0.0)
        high = jnp.where(jnp.logical_and(hit, second), 1.0, 0.0)
        picked = jnp.dot(
            low.astype(jnp.bfloat16), window, preferred_element_type=jnp.float32
        ) + pltpu.roll(
            jnp.dot(high.astype(jnp.bfloat16), window, preferred_element_type=jnp.float32), 64, 1
        )
        result = lax.dot_general(
            picked.astype(jnp.bfloat16),
            rows,
            (((0,), (0,)), ((), ())),
            preferred_element_type=jnp.float32,
        )
        return result[:load_count]

    local = smoothed_ref[...].astype(jnp.float32) - near_smoothed_ref[...].astype(jnp.float32)
    direction = local + lifted(0, modes_ref[...])
    near_lifted = jnp.concatenate(
        [
            lifted(1, near_modes_ref[:, :face]),
            lifted(2, near_modes_ref[:, face : 2 * face]),
            lifted(3, near_modes_ref[:, 2 * face :]),
        ],
        axis=1,
    )
    near = near_lifted - exists_ref[...] * local
    if len(refs) > 8:
        ratio_ref, previous_ref, near_previous_ref = refs[5:8]
        ratio = ratio_ref[...]
        direction += ratio * previous_ref[...]
        near += ratio * near_previous_ref[...]
    out_ref[...] = direction
    near_ref[...] = near
    moved_ref[...] = (
        direction.astype(jnp.bfloat16).astype(jnp.float32)
        - near.astype(jnp.bfloat16).astype(jnp.float32)
    ).astype(jnp.bfloat16)


def next_direction(info, blocks, modes, near_modes, smoothed, near_smoothed, exists, *previous):
    rest = (modes, near_modes, smoothed, near_smoothed, exists) + previous
    shape = smoothed.shape
    in_vmem = pl.BlockSpec(memory_space=pltpu.VMEM)
    return pl.pallas_call(
        direction_kernel,
        out_shape=(
            jax.ShapeDtypeStruct(shape, jnp.float32),
            jax.ShapeDtypeStruct(shape, jnp.float32),
            jax.ShapeDtypeStruct(shape, jnp.bfloat16),
        ),
        in_specs=[pl.BlockSpec(memory_space=pltpu.SMEM)] + [in_vmem] * (1 + len(rest)),
        out_specs=(in_vmem,) * 3,
        interpret=INTERPRET,
        compiler_params=pltpu.CompilerParams(vmem_limit_bytes=8 << 20),
        name="next_direction",
    )(info, blocks, *rest)


def shards(loads, flexibility, dirichlet, modes, coarse_inverse, mode_counts):
    local_loads = loads[0, 0]
    flex_block = flexibility[0, 0]
    precond_block = dirichlet[0, 0]
    mode_block = modes[0, 0]
    nx, nz, ny = XYZ
    rows = lax.axis_size(WIDE)
    row = lax.axis_index(WIDE)
    column = lax.axis_index("c")
    column_width = coarse_inverse.shape[1]
    face = local_loads.shape[1] // 4

    has_neighbour = jnp.stack([row > 0, row < rows - 1, column == 1, column == 0])
    exists = jnp.repeat(jnp.where(has_neighbour, 1.0, 0.0), face)[None, :]
    factor = 1.0 + exists

    def weigh(rounded):
        return lax.dot_general(
            mode_block, rounded, (((1,), (1,)), ((), ())), preferred_element_type=jnp.float32
        )

    def smooth(rounded):
        inner = (rounded.astype(jnp.float32) * factor).astype(jnp.bfloat16)
        return jnp.dot(inner, precond_block, preferred_element_type=jnp.float32).astype(
            jnp.bfloat16
        )

    def apply_flex(values):
        return jnp.dot(values, flex_block, preferred_element_type=jnp.float32).astype(jnp.bfloat16)

    def load_dot(left, right):
        return jnp.sum(left.astype(jnp.float32) * right.astype(jnp.float32), axis=1)

    residual = jump(apply_flex(local_loads))
    rounded = residual.astype(jnp.bfloat16)
    payload = pack(weigh(rounded).astype(jnp.bfloat16))
    payload, mode_counts = lax.optimization_barrier((payload, mode_counts))
    stage = along_z(payload)

    all_ends = jnp.cumsum(mode_counts, axis=1)
    all_starts = all_ends - mode_counts
    own_first = column == 0
    counts = jnp.where(own_first, mode_counts[0], mode_counts[1])
    starts = jnp.where(own_first, all_starts[0], all_starts[1])
    padded = padded_inverse(coarse_inverse, starts, counts, 32 * row - column * column_width)

    column_of = jnp.stack([column, column, column, 1 - column])
    row_of = jnp.stack([row, row - 1, row + 1, row])
    chosen = jnp.logical_and(
        jnp.arange(rows)[None, None, :] == row_of[:, None, None],
        jnp.arange(2)[None, :, None] == column_of[:, None, None],
    )
    start_of = jnp.sum(jnp.where(chosen, all_starts[None], 0), axis=(1, 2))
    count_of = jnp.sum(jnp.where(chosen, mode_counts[None], 0), axis=(1, 2))
    base = column_of * column_width + start_of
    owner = jnp.minimum(base // 32, rows - 2)

    def place(chip):
        return (chip // (ny * nz)) * (ny * nz) + (chip % ny) * nz + (chip // ny) % nz

    info = jnp.stack([place(owner), place(owner + 1), base - 32 * owner, count_of], axis=1)
    info = info.reshape(-1).astype(jnp.int32)

    stage, padded, info, rounded = lax.optimization_barrier((stage, padded, info, rounded))
    smoothed = smooth(rounded)
    near_smoothed = neighbours(smoothed)
    blocks, near_smoothed, late_modes = lax.optimization_barrier(
        (across(stage), near_smoothed, mode_block)
    )
    near_modes = neighbours(late_modes)
    first_sums = swapped_sum(coarse_product(padded, blocks))
    half_slots = first_sums.shape[0] // 2
    values = across(along_z(first_sums[:half_slots].astype(jnp.bfloat16)))
    direction, near_direction, moved = next_direction(
        info, values, mode_block, near_modes, smoothed, near_smoothed, exists
    )

    pushed = apply_flex(moved)
    partials = jnp.concatenate([load_dot(residual, direction), load_dot(moved, pushed)])[None, :]
    image = jump(pushed)
    image_high = lax.reduce_precision(image, 8, 7)
    image_low = (image - image_high).astype(jnp.bfloat16)
    image_weights = weigh(image_high.astype(jnp.bfloat16)) + weigh(image_low)
    blocks = gather_with_sum(pack(image_weights.astype(jnp.bfloat16)), partials)
    second_sums = swapped_sum(coarse_product(padded, blocks))
    totals = jnp.sum(second_sums[2 * half_slots :], axis=0)
    energy = totals[:64]
    size = energy / totals[64:]
    multipliers = size[:, None] * direction
    residual = residual - size[:, None] * image

    packed = first_sums - jnp.tile(size, 2)[None, :] * second_sums[: 2 * half_slots]
    rounded = residual.astype(jnp.bfloat16)
    smoothed = smooth(rounded)
    coarse_values = lax.reduce_precision(packed[:half_slots], 8, 7)
    coarse_energy = jnp.sum(coarse_values * packed[half_slots:], axis=0)
    local_energy = load_dot(residual * factor, smoothed)
    partial = local_energy + 0.5 * (coarse_energy[:64] + coarse_energy[64:])
    partial = jnp.concatenate([partial, jnp.zeros_like(partial)])[None, :]
    near_smoothed = neighbours(smoothed)
    values = gather_with_sum(coarse_values.astype(jnp.bfloat16), partial)
    sums = jnp.sum(values[:, nz * half_slots :, :].astype(jnp.float32), axis=(0, 1))[None, :]
    fresh = swapped_sum(sums)[0, :64]
    direction, near_direction, moved = next_direction(
        info,
        values,
        mode_block,
        near_modes,
        smoothed,
        near_smoothed,
        exists,
        (fresh / energy)[:, None],
        direction,
        near_direction,
    )

    pushed = apply_flex(moved)
    curvature = total(load_dot(moved, pushed)[None, :])[0]
    image = jump(pushed)
    size = (fresh / curvature)[:, None]
    multipliers = multipliers + size * direction
    residual = residual - size * image
    return (multipliers.astype(jnp.bfloat16)[None, None], residual.astype(jnp.bfloat16)[None, None])


def solution(mesh):
    split = Mesh(mesh.devices.reshape(XYZ + (2,)), WIDE + ("c",))
    blocks = P(WIDE, "c", None, None)
    return jax.shard_map(
        shards,
        mesh=split,
        in_specs=(blocks, blocks, blocks, blocks, P(WIDE, "c"), P()),
        out_specs=(blocks, blocks),
        check_vma=False,
    )
```

```python
import jax
import jax.numpy as jnp
from jax import lax
from jax.experimental import pallas as pl
from jax.experimental.pallas import tpu as pltpu
from jax.sharding import Mesh, PartitionSpec as P


XYZ = (4, 16, 4)
WIDE = ("x", "z", "y")
INTERPRET = False


def spread(values, axes):
    count = lax.axis_size(axes)
    copies = jnp.broadcast_to(values[None], (count,) + values.shape)
    return lax.all_to_all(copies, axes, 0, 0, tiled=False)


def along_z(block):
    return spread(block, "z").reshape(-1, block.shape[1])


def across(block):
    return spread(block, ("x", "y"))


def with_sum(block, partial):
    return jnp.concatenate([block, in_pieces(partial)], axis=0)


def summed_along_z(payload):
    stage = spread(payload, "z")
    rows = payload.shape[0] - 8
    sums = jnp.sum(stage[:, rows:, :].astype(jnp.float32), axis=(0, 1))[None, :]
    return with_sum(stage[:, :rows, :].reshape(-1, payload.shape[1]), sums)


def total(partial):
    stage = jnp.sum(spread(partial, ("x", "y", "c")), axis=0)
    return jnp.sum(spread(stage, "z"), axis=0)


def neighbours(values):
    _, width = values.shape
    face = width // 4
    rows = lax.axis_size(WIDE)
    column = lax.axis_index("c")
    down = [(i, i + 1) for i in range(rows - 1)]
    up = [(i + 1, i) for i in range(rows - 1)]
    north, south, west, east = (values[:, k * face : (k + 1) * face] for k in range(4))
    from_above = lax.ppermute(south, WIDE, down)
    from_below = lax.ppermute(north, WIDE, up)
    side = lax.ppermute(jnp.where(column == 0, east, west), "c", [(0, 1), (1, 0)])
    nothing = jnp.zeros_like(side)
    from_west = jnp.where(column == 1, side, nothing)
    from_east = jnp.where(column == 0, side, nothing)
    return jnp.concatenate([from_above, from_below, from_west, from_east], axis=1)


def jump(values):
    return values.astype(jnp.float32) - neighbours(values).astype(jnp.float32)


def pack(wide_rows):
    half = wide_rows.shape[0] // 2
    return jnp.concatenate([wide_rows[:half], wide_rows[half:]], axis=1)


def pad_kernel(first_ref, source_ref, block_ref, out_ref):
    rows, columns = block_ref.shape
    window = min(384, columns)
    chunks = out_ref.shape[1] // 128
    position = lax.broadcasted_iota(jnp.int32, (window, 128), 0)
    own_row = lax.broadcasted_iota(jnp.int32, (rows, window), 0) + first_ref[chunks]
    own_column = lax.broadcasted_iota(jnp.int32, (rows, window), 1)

    def step(chunk, carry):
        low = pl.multiple_of(first_ref[chunk] * 128, 128)
        unit = jnp.where(own_column + low == own_row, 1.0, 0.0).astype(jnp.bfloat16)
        part = jnp.concatenate([block_ref[:, pl.ds(low, window)], unit], axis=0)
        target = pl.multiple_of(chunk * 128, 128)
        for half in range(2):
            hot = jnp.where(position == source_ref[half, chunk] - low, 1.0, 0.0).astype(jnp.bfloat16)
            chosen = jnp.dot(part, hot, preferred_element_type=jnp.float32)
            out_ref[2 * half * rows : 2 * (half + 1) * rows, pl.ds(target, 128)] = chosen.astype(
                jnp.bfloat16
            )
        return carry

    lax.fori_loop(0, chunks, step, 0)


def padded_inverse(block, starts, counts, own_first):
    rows, columns = block.shape
    subdomains = counts.shape[0]
    slots = 32
    half_slots = slots // 2
    rank = jnp.arange(slots, dtype=jnp.int32)
    source = jnp.where(rank[None, :] < counts[:, None], starts[:, None] + rank[None, :], -1)
    chunks = subdomains * half_slots // 128
    source = source.reshape(subdomains, 2, half_slots).transpose(1, 0, 2).reshape(2, chunks, 1, 128)
    window = min(384, columns)
    first = jnp.minimum(starts.reshape(chunks, -1)[:, 0] // 128, (columns - window) // 128)
    first = jnp.concatenate([first, own_first[None]])
    return pl.pallas_call(
        pad_kernel,
        out_shape=jax.ShapeDtypeStruct((4 * rows, subdomains * half_slots), jnp.bfloat16),
        in_specs=[
            pl.BlockSpec(memory_space=pltpu.SMEM),
            pl.BlockSpec(memory_space=pltpu.VMEM),
            pl.BlockSpec(memory_space=pltpu.VMEM),
        ],
        out_specs=pl.BlockSpec(memory_space=pltpu.VMEM),
        interpret=INTERPRET,
        compiler_params=pltpu.CompilerParams(vmem_limit_bytes=8 << 20),
        name="pad_inverse",
    )(first, source, block)


def product_kernel(padded_ref, blocks_ref, out_ref):
    nx, nz, ny = XYZ
    rows = padded_ref.shape[0] // 4
    half = rows // 2
    length = nz * ny * half
    result = jnp.zeros((4 * rows, 128), jnp.float32)
    for x in range(nx):
        order = [(x * ny + y, z * half) for z in range(nz) for y in range(ny)]
        part = jnp.concatenate([blocks_ref[p, r : r + half, :] for p, r in order], axis=0)
        result += jnp.dot(
            padded_ref[:, x * length : (x + 1) * length], part, preferred_element_type=jnp.float32
        )
    joined = result[: 2 * rows] + pltpu.roll(result[2 * rows :], 64, 1)
    lane = lax.broadcasted_iota(jnp.int32, (half, 128), 1)
    for k in range(2):
        low = joined[2 * k * half : (2 * k + 1) * half]
        high = joined[(2 * k + 1) * half : (2 * k + 2) * half]
        out_ref[k * half : (k + 1) * half, :] = jnp.where(lane < 64, low, pltpu.roll(high, 64, 1))
    if out_ref.shape[0] > rows:
        sums = jnp.zeros((8, 128), jnp.float32)
        for p in range(blocks_ref.shape[0]):
            sums += blocks_ref[p, nz * half : nz * half + 8, :].astype(jnp.float32)
        out_ref[rows : rows + 8, :] = sums


def coarse_product(padded, blocks):
    rows = padded.shape[0] // 4
    return pl.pallas_call(
        product_kernel,
        out_shape=jax.ShapeDtypeStruct((rows + blocks.shape[1] - XYZ[1] * (rows // 2), 128), jnp.float32),
        in_specs=[pl.BlockSpec(memory_space=pltpu.VMEM)] * 2,
        out_specs=pl.BlockSpec(memory_space=pltpu.VMEM),
        interpret=INTERPRET,
        compiler_params=pltpu.CompilerParams(vmem_limit_bytes=8 << 20),
        name="coarse_product",
    )(padded, blocks)


def in_pieces(values):
    rest = values
    pieces = []
    for _ in range(3):
        piece = lax.reduce_precision(rest, 8, 7)
        pieces.append(piece)
        rest = rest - piece
    pieces.append(jnp.zeros((8 - len(pieces), values.shape[1]), jnp.float32))
    return jnp.concatenate(pieces, axis=0).astype(jnp.bfloat16)


def swapped_sum(partial):
    return partial + lax.ppermute(partial, "c", [(0, 1), (1, 0)])


def direction_kernel(info_ref, blocks_ref, exists_ref, *refs):
    copied = (len(refs) - 4) // 2 if len(refs) % 2 == 0 else (len(refs) - 5) // 2
    sources, buffers, semaphores = refs[:copied], refs[-1 - copied : -1], refs[-1]
    out_ref, near_ref, moved_ref = refs[-4 - copied : -1 - copied]
    copies = [
        pltpu.make_async_copy(source, buffer, semaphores.at[k])
        for k, (source, buffer) in enumerate(zip(sources, buffers))
    ]
    for copy in copies:
        copy.start()
    modes_ref, near_modes_ref, smoothed_ref, near_smoothed_ref = buffers[:4]
    slots, width = modes_ref.shape
    load_count = out_ref.shape[0]
    face = width // 4
    half_slots = slots // 2
    rank = lax.broadcasted_iota(jnp.int32, (slots, slots), 0)
    column = lax.broadcasted_iota(jnp.int32, (slots, slots), 1)

    def chip_block(chip):
        start = pl.multiple_of((chip % XYZ[1]) * half_slots, half_slots)
        return blocks_ref[chip // XYZ[1], pl.ds(start, half_slots), :]

    def picked(which):
        window = jnp.concatenate(
            [chip_block(info_ref[4 * which]), chip_block(info_ref[4 * which + 1])], axis=0
        )
        offset = info_ref[4 * which + 2] + rank
        row = (offset // slots) * half_slots + offset % half_slots
        second = (offset // half_slots) % 2 == 1
        hit = jnp.logical_and(row == column, rank < info_ref[4 * which + 3])
        low = jnp.where(jnp.logical_and(hit, jnp.logical_not(second)), 1.0, 0.0)
        high = jnp.where(jnp.logical_and(hit, second), 1.0, 0.0)
        return (
            jnp.dot(low.astype(jnp.bfloat16), window, preferred_element_type=jnp.float32)
            + pltpu.roll(
                jnp.dot(high.astype(jnp.bfloat16), window, preferred_element_type=jnp.float32), 64, 1
            )
        ).astype(jnp.bfloat16)

    def lifted(values, rows):
        result = lax.dot_general(
            values, rows, (((0,), (0,)), ((), ())), preferred_element_type=jnp.float32
        )
        return result[:load_count]

    chosen = [picked(which) for which in range(4)]
    for copy in copies:
        copy.wait()
    local = smoothed_ref[...].astype(jnp.float32) - near_smoothed_ref[...].astype(jnp.float32)
    direction = local + lifted(chosen[0], modes_ref[...])
    near_lifted = jnp.concatenate(
        [
            lifted(chosen[1], near_modes_ref[:, :face]),
            lifted(chosen[2], near_modes_ref[:, face : 2 * face]),
            lifted(chosen[3], near_modes_ref[:, 2 * face :]),
        ],
        axis=1,
    )
    near = near_lifted - exists_ref[...] * local
    if copied > 4:
        previous_ref, near_previous_ref = buffers[4:]
        ratio = refs[copied][...]
        direction += ratio * previous_ref[...]
        near += ratio * near_previous_ref[...]
    out_ref[...] = direction
    near_ref[...] = near
    moved_ref[...] = (
        direction.astype(jnp.bfloat16).astype(jnp.float32)
        - near.astype(jnp.bfloat16).astype(jnp.float32)
    ).astype(jnp.bfloat16)


def next_direction(
    info, blocks, exists, modes, near_modes, smoothed, near_smoothed, ratio=None, previous=()
):
    copied = (modes, near_modes, smoothed, near_smoothed) + previous
    ratios = () if ratio is None else (ratio,)
    shape = smoothed.shape
    in_vmem = pl.BlockSpec(memory_space=pltpu.VMEM)
    return pl.pallas_call(
        direction_kernel,
        out_shape=(
            jax.ShapeDtypeStruct(shape, jnp.float32),
            jax.ShapeDtypeStruct(shape, jnp.float32),
            jax.ShapeDtypeStruct(shape, jnp.bfloat16),
        ),
        in_specs=[pl.BlockSpec(memory_space=pltpu.SMEM), in_vmem, in_vmem]
        + [pl.BlockSpec(memory_space=pltpu.HBM)] * len(copied)
        + [in_vmem] * len(ratios),
        out_specs=(in_vmem,) * 3,
        scratch_shapes=[pltpu.VMEM(array.shape, array.dtype) for array in copied]
        + [pltpu.SemaphoreType.DMA((len(copied),))],
        interpret=INTERPRET,
        compiler_params=pltpu.CompilerParams(vmem_limit_bytes=8 << 20),
        name="next_direction",
    )(info, blocks, exists, *copied, *ratios)


def shards(loads, flexibility, dirichlet, modes, coarse_inverse, mode_counts):
    local_loads = loads[0, 0]
    flex_block = flexibility[0, 0]
    precond_block = dirichlet[0, 0]
    mode_block = modes[0, 0]
    _, nz, ny = XYZ
    rows = lax.axis_size(WIDE)
    row = lax.axis_index(WIDE)
    column = lax.axis_index("c")
    column_width = coarse_inverse.shape[1]
    face = local_loads.shape[1] // 4

    has_neighbour = jnp.stack([row > 0, row < rows - 1, column == 1, column == 0])
    exists = jnp.repeat(jnp.where(has_neighbour, 1.0, 0.0), face)[None, :]
    factor = 1.0 + exists

    def weigh(rounded):
        return lax.dot_general(
            mode_block, rounded, (((1,), (1,)), ((), ())), preferred_element_type=jnp.float32
        )

    def smooth(rounded):
        inner = (rounded.astype(jnp.float32) * factor).astype(jnp.bfloat16)
        return jnp.dot(inner, precond_block, preferred_element_type=jnp.float32).astype(
            jnp.bfloat16
        )

    def apply_flex(values):
        return jnp.dot(values, flex_block, preferred_element_type=jnp.float32).astype(jnp.bfloat16)

    def load_dot(left, right):
        return jnp.sum(left.astype(jnp.float32) * right.astype(jnp.float32), axis=1)

    residual = jump(apply_flex(local_loads))
    rounded = residual.astype(jnp.bfloat16)
    payload = pack(weigh(rounded).astype(jnp.bfloat16))
    payload, mode_counts, late_modes = lax.optimization_barrier((payload, mode_counts, mode_block))
    stage = along_z(payload)
    near_modes = neighbours(late_modes)

    all_ends = jnp.cumsum(mode_counts, axis=1)
    all_starts = all_ends - mode_counts
    own_first = column == 0
    counts = jnp.where(own_first, mode_counts[0], mode_counts[1])
    starts = jnp.where(own_first, all_starts[0], all_starts[1])
    padded = padded_inverse(coarse_inverse, starts, counts, 32 * row - column * column_width)

    column_of = jnp.stack([column, column, column, 1 - column])
    row_of = jnp.stack([row, row - 1, row + 1, row])
    chosen = jnp.logical_and(
        jnp.arange(rows)[None, None, :] == row_of[:, None, None],
        jnp.arange(2)[None, :, None] == column_of[:, None, None],
    )
    start_of = jnp.sum(jnp.where(chosen, all_starts[None], 0), axis=(1, 2))
    count_of = jnp.sum(jnp.where(chosen, mode_counts[None], 0), axis=(1, 2))
    base = column_of * column_width + start_of
    owner = jnp.minimum(base // 32, rows - 2)

    def place(chip):
        return (chip // (ny * nz)) * (ny * nz) + (chip % ny) * nz + (chip // ny) % nz

    info = jnp.stack([place(owner), place(owner + 1), base - 32 * owner, count_of], axis=1)
    info = info.reshape(-1).astype(jnp.int32)

    stage, padded, info, rounded = lax.optimization_barrier((stage, padded, info, rounded))
    smoothed = smooth(rounded)
    near_smoothed = neighbours(smoothed)
    blocks = across(stage)
    products = coarse_product(padded, blocks)
    first_sums = swapped_sum(products)
    half_slots = first_sums.shape[0] // 2
    stage = along_z(first_sums[:half_slots].astype(jnp.bfloat16))
    stage, near_smoothed = lax.optimization_barrier((stage, near_smoothed))
    values = across(stage)
    direction, near_direction, moved = next_direction(
        info, values, exists, mode_block, near_modes, smoothed, near_smoothed
    )

    pushed = apply_flex(moved)
    partials = jnp.concatenate([load_dot(residual, direction), load_dot(moved, pushed)])[None, :]
    image = jump(pushed)
    image_high = lax.reduce_precision(image, 8, 7)
    image_low = (image - image_high).astype(jnp.bfloat16)
    image_weights = weigh(image_high.astype(jnp.bfloat16)) + weigh(image_low)
    payload = with_sum(pack(image_weights.astype(jnp.bfloat16)), partials)
    payload, late_image = lax.optimization_barrier((payload, image))
    stage = summed_along_z(payload)
    image_smoothed = smooth(late_image.astype(jnp.bfloat16))
    residual_jump, image_jump = residual * factor, late_image * factor
    energies = (
        load_dot(residual_jump, smoothed),
        load_dot(residual_jump, image_smoothed) + load_dot(image_jump, smoothed),
        load_dot(image_jump, image_smoothed),
    )
    stage, energies = lax.optimization_barrier((stage, energies))
    second_sums = swapped_sum(coarse_product(padded, across(stage)))
    totals = jnp.sum(second_sums[2 * half_slots :], axis=0)
    energy = totals[:64]
    size = energy / totals[64:]
    local_energy = energies[0] - size * (energies[1] - size * energies[2])

    packed = first_sums - jnp.tile(size, 2)[None, :] * second_sums[: 2 * half_slots]
    coarse_values = lax.reduce_precision(packed[:half_slots], 8, 7)
    coarse_energy = jnp.sum(coarse_values * packed[half_slots:], axis=0)
    partial = local_energy + 0.5 * (coarse_energy[:64] + coarse_energy[64:])
    partial = jnp.concatenate([partial, jnp.zeros_like(partial)])[None, :]
    payload = with_sum(coarse_values.astype(jnp.bfloat16), partial)
    payload, size = lax.optimization_barrier((payload, size))
    multipliers = size[:, None] * direction
    residual = residual - size[:, None] * image
    smoothed = smooth(residual.astype(jnp.bfloat16))
    near_smoothed = neighbours(smoothed)
    stage = summed_along_z(payload)
    stage, smoothed = lax.optimization_barrier((stage, smoothed))
    values = across(stage)
    sums = jnp.sum(values[:, nz * half_slots :, :].astype(jnp.float32), axis=(0, 1))[None, :]
    fresh = swapped_sum(sums)[0, :64]
    direction, near_direction, moved = next_direction(
        info,
        values,
        exists,
        mode_block,
        near_modes,
        smoothed,
        near_smoothed,
        (fresh / energy)[:, None],
        (direction, near_direction),
    )

    pushed = apply_flex(moved)
    curvature = total(load_dot(moved, pushed)[None, :])[0]
    image = jump(pushed)
    size = (fresh / curvature)[:, None]
    multipliers = multipliers + size * direction
    residual = residual - size * image
    return (multipliers.astype(jnp.bfloat16)[None, None], residual.astype(jnp.bfloat16)[None, None])


def solution(mesh):
    split = Mesh(mesh.devices.reshape(XYZ + (2,)), WIDE + ("c",))
    blocks = P(WIDE, "c", None, None)
    return jax.shard_map(
        shards,
        mesh=split,
        in_specs=(blocks, blocks, blocks, blocks, P(WIDE, "c"), P()),
        out_specs=(blocks, blocks),
        check_vma=False,
    )
```

```python
import jax
import jax.numpy as jnp
from jax import lax
from jax.experimental import pallas as pl
from jax.experimental.pallas import tpu as pltpu
from jax.sharding import Mesh, PartitionSpec as P


XYZ = (4, 16, 4)
WIDE = ("x", "z", "y")
INTERPRET = False


def spread(values, axes):
    count = lax.axis_size(axes)
    copies = jnp.broadcast_to(values[None], (count,) + values.shape)
    return lax.all_to_all(copies, axes, 0, 0, tiled=False)


def along_z(block):
    return spread(block, "z").reshape(-1, block.shape[1])


def across(block):
    return spread(block, ("x", "y"))


def with_sum(block, partial):
    return jnp.concatenate([block, in_pieces(partial)], axis=0)


def summed_along_z(payload):
    stage = spread(payload, "z")
    rows = payload.shape[0] - 8
    sums = jnp.sum(stage[:, rows:, :].astype(jnp.float32), axis=(0, 1))[None, :]
    return with_sum(stage[:, :rows, :].reshape(-1, payload.shape[1]), sums)


def total(partial):
    stage = jnp.sum(spread(partial, ("x", "y", "c")), axis=0)
    return jnp.sum(spread(stage, "z"), axis=0)


def neighbours(values):
    _, width = values.shape
    face = width // 4
    rows = lax.axis_size(WIDE)
    column = lax.axis_index("c")
    down = [(i, i + 1) for i in range(rows - 1)]
    up = [(i + 1, i) for i in range(rows - 1)]
    north, south, west, east = (values[:, k * face : (k + 1) * face] for k in range(4))
    from_above = lax.ppermute(south, WIDE, down)
    from_below = lax.ppermute(north, WIDE, up)
    side = lax.ppermute(jnp.where(column == 0, east, west), "c", [(0, 1), (1, 0)])
    nothing = jnp.zeros_like(side)
    from_west = jnp.where(column == 1, side, nothing)
    from_east = jnp.where(column == 0, side, nothing)
    return jnp.concatenate([from_above, from_below, from_west, from_east], axis=1)


def jump(values):
    return values.astype(jnp.float32) - neighbours(values).astype(jnp.float32)


def pack(wide_rows):
    half = wide_rows.shape[0] // 2
    return jnp.concatenate([wide_rows[:half], wide_rows[half:]], axis=1)


def pad_kernel(first_ref, source_ref, block_ref, out_ref):
    rows, columns = block_ref.shape
    window = min(384, columns)
    chunks = out_ref.shape[1] // 128
    position = lax.broadcasted_iota(jnp.int32, (window, 128), 0)
    own_row = lax.broadcasted_iota(jnp.int32, (rows, window), 0) + first_ref[chunks]
    own_column = lax.broadcasted_iota(jnp.int32, (rows, window), 1)

    def step(chunk, carry):
        low = pl.multiple_of(first_ref[chunk] * 128, 128)
        unit = jnp.where(own_column + low == own_row, 1.0, 0.0).astype(jnp.bfloat16)
        part = jnp.concatenate([block_ref[:, pl.ds(low, window)], unit], axis=0)
        target = pl.multiple_of(chunk * 128, 128)
        for half in range(2):
            hot = jnp.where(position == source_ref[half, chunk] - low, 1.0, 0.0).astype(jnp.bfloat16)
            chosen = jnp.dot(part, hot, preferred_element_type=jnp.float32)
            out_ref[2 * half * rows : 2 * (half + 1) * rows, pl.ds(target, 128)] = chosen.astype(
                jnp.bfloat16
            )
        return carry

    lax.fori_loop(0, chunks, step, 0)


def padded_inverse(block, starts, counts, own_first):
    rows, columns = block.shape
    subdomains = counts.shape[0]
    slots = 32
    half_slots = slots // 2
    rank = jnp.arange(slots, dtype=jnp.int32)
    source = jnp.where(rank[None, :] < counts[:, None], starts[:, None] + rank[None, :], -1)
    chunks = subdomains * half_slots // 128
    source = source.reshape(subdomains, 2, half_slots).transpose(1, 0, 2).reshape(2, chunks, 1, 128)
    window = min(384, columns)
    first = jnp.minimum(starts.reshape(chunks, -1)[:, 0] // 128, (columns - window) // 128)
    first = jnp.concatenate([first, own_first[None]])
    return pl.pallas_call(
        pad_kernel,
        out_shape=jax.ShapeDtypeStruct((4 * rows, subdomains * half_slots), jnp.bfloat16),
        in_specs=[
            pl.BlockSpec(memory_space=pltpu.SMEM),
            pl.BlockSpec(memory_space=pltpu.VMEM),
            pl.BlockSpec(memory_space=pltpu.VMEM),
        ],
        out_specs=pl.BlockSpec(memory_space=pltpu.VMEM),
        interpret=INTERPRET,
        compiler_params=pltpu.CompilerParams(vmem_limit_bytes=8 << 20),
        name="pad_inverse",
    )(first, source, block)


def product_kernel(padded_ref, blocks_ref, out_ref):
    nx, nz, ny = XYZ
    rows = padded_ref.shape[0] // 4
    half = rows // 2
    length = nz * ny * half
    result = jnp.zeros((4 * rows, 128), jnp.float32)
    for x in range(nx):
        order = [(x * ny + y, z * half) for z in range(nz) for y in range(ny)]
        part = jnp.concatenate([blocks_ref[p, r : r + half, :] for p, r in order], axis=0)
        result += jnp.dot(
            padded_ref[:, x * length : (x + 1) * length], part, preferred_element_type=jnp.float32
        )
    joined = result[: 2 * rows] + pltpu.roll(result[2 * rows :], 64, 1)
    lane = lax.broadcasted_iota(jnp.int32, (half, 128), 1)
    for k in range(2):
        low = joined[2 * k * half : (2 * k + 1) * half]
        high = joined[(2 * k + 1) * half : (2 * k + 2) * half]
        out_ref[k * half : (k + 1) * half, :] = jnp.where(lane < 64, low, pltpu.roll(high, 64, 1))
    if out_ref.shape[0] > rows:
        sums = jnp.zeros((8, 128), jnp.float32)
        for p in range(blocks_ref.shape[0]):
            sums += blocks_ref[p, nz * half : nz * half + 8, :].astype(jnp.float32)
        out_ref[rows : rows + 8, :] = sums


def coarse_product(padded, blocks):
    rows = padded.shape[0] // 4
    return pl.pallas_call(
        product_kernel,
        out_shape=jax.ShapeDtypeStruct((rows + blocks.shape[1] - XYZ[1] * (rows // 2), 128), jnp.float32),
        in_specs=[pl.BlockSpec(memory_space=pltpu.VMEM)] * 2,
        out_specs=pl.BlockSpec(memory_space=pltpu.VMEM),
        interpret=INTERPRET,
        compiler_params=pltpu.CompilerParams(vmem_limit_bytes=8 << 20),
        name="coarse_product",
    )(padded, blocks)


def in_pieces(values):
    rest = values
    pieces = []
    for _ in range(3):
        piece = lax.reduce_precision(rest, 8, 7)
        pieces.append(piece)
        rest = rest - piece
    pieces.append(jnp.zeros((8 - len(pieces), values.shape[1]), jnp.float32))
    return jnp.concatenate(pieces, axis=0).astype(jnp.bfloat16)


def swapped_sum(partial):
    return partial + lax.ppermute(partial, "c", [(0, 1), (1, 0)])


def direction_kernel(info_ref, blocks_ref, *refs):
    modes_ref, near_modes_ref, smoothed_ref, near_smoothed_ref, exists_ref = refs[:5]
    out_ref, near_ref, moved_ref = refs[-3:]
    slots, width = modes_ref.shape
    load_count = out_ref.shape[0]
    face = width // 4
    half_slots = slots // 2
    rank = lax.broadcasted_iota(jnp.int32, (slots, slots), 0)
    column = lax.broadcasted_iota(jnp.int32, (slots, slots), 1)

    def chip_block(chip):
        start = pl.multiple_of((chip % XYZ[1]) * half_slots, half_slots)
        return blocks_ref[chip // XYZ[1], pl.ds(start, half_slots), :]

    def lifted(which, rows):
        window = jnp.concatenate(
            [chip_block(info_ref[4 * which]), chip_block(info_ref[4 * which + 1])], axis=0
        )
        offset = info_ref[4 * which + 2] + rank
        row = (offset // slots) * half_slots + offset % half_slots
        second = (offset // half_slots) % 2 == 1
        hit = jnp.logical_and(row == column, rank < info_ref[4 * which + 3])
        low = jnp.where(jnp.logical_and(hit, jnp.logical_not(second)), 1.0, 0.0)
        high = jnp.where(jnp.logical_and(hit, second), 1.0, 0.0)
        picked = jnp.dot(
            low.astype(jnp.bfloat16), window, preferred_element_type=jnp.float32
        ) + pltpu.roll(
            jnp.dot(high.astype(jnp.bfloat16), window, preferred_element_type=jnp.float32), 64, 1
        )
        result = lax.dot_general(
            picked.astype(jnp.bfloat16),
            rows,
            (((0,), (0,)), ((), ())),
            preferred_element_type=jnp.float32,
        )
        return result[:load_count]

    local = smoothed_ref[...].astype(jnp.float32) - near_smoothed_ref[...].astype(jnp.float32)
    direction = local + lifted(0, modes_ref[...])
    near_lifted = jnp.concatenate(
        [
            lifted(1, near_modes_ref[:, :face]),
            lifted(2, near_modes_ref[:, face : 2 * face]),
            lifted(3, near_modes_ref[:, 2 * face :]),
        ],
        axis=1,
    )
    near = near_lifted - exists_ref[...] * local
    if len(refs) > 8:
        ratio_ref, previous_ref, near_previous_ref = refs[5:8]
        ratio = ratio_ref[...]
        direction += ratio * previous_ref[...]
        near += ratio * near_previous_ref[...]
    out_ref[...] = direction
    near_ref[...] = near
    moved_ref[...] = (
        direction.astype(jnp.bfloat16).astype(jnp.float32)
        - near.astype(jnp.bfloat16).astype(jnp.float32)
    ).astype(jnp.bfloat16)


def next_direction(info, blocks, modes, near_modes, smoothed, near_smoothed, exists, *previous):
    rest = (modes, near_modes, smoothed, near_smoothed, exists) + previous
    shape = smoothed.shape
    in_vmem = pl.BlockSpec(memory_space=pltpu.VMEM)
    return pl.pallas_call(
        direction_kernel,
        out_shape=(
            jax.ShapeDtypeStruct(shape, jnp.float32),
            jax.ShapeDtypeStruct(shape, jnp.float32),
            jax.ShapeDtypeStruct(shape, jnp.bfloat16),
        ),
        in_specs=[pl.BlockSpec(memory_space=pltpu.SMEM)] + [in_vmem] * (1 + len(rest)),
        out_specs=(in_vmem,) * 3,
        interpret=INTERPRET,
        compiler_params=pltpu.CompilerParams(vmem_limit_bytes=8 << 20),
        name="next_direction",
    )(info, blocks, *rest)


def shards(loads, flexibility, dirichlet, modes, coarse_inverse, mode_counts):
    local_loads = loads[0, 0]
    flex_block = flexibility[0, 0]
    precond_block = dirichlet[0, 0]
    mode_block = modes[0, 0]
    _, nz, ny = XYZ
    rows = lax.axis_size(WIDE)
    row = lax.axis_index(WIDE)
    column = lax.axis_index("c")
    column_width = coarse_inverse.shape[1]
    face = local_loads.shape[1] // 4

    has_neighbour = jnp.stack([row > 0, row < rows - 1, column == 1, column == 0])
    exists = jnp.repeat(jnp.where(has_neighbour, 1.0, 0.0), face)[None, :]
    factor = 1.0 + exists

    def weigh(rounded):
        return lax.dot_general(
            mode_block, rounded, (((1,), (1,)), ((), ())), preferred_element_type=jnp.float32
        )

    def smooth(rounded):
        inner = (rounded.astype(jnp.float32) * factor).astype(jnp.bfloat16)
        return jnp.dot(inner, precond_block, preferred_element_type=jnp.float32).astype(
            jnp.bfloat16
        )

    def apply_flex(values):
        return jnp.dot(values, flex_block, preferred_element_type=jnp.float32).astype(jnp.bfloat16)

    def load_dot(left, right):
        return jnp.sum(left.astype(jnp.float32) * right.astype(jnp.float32), axis=1)

    load_count = local_loads.shape[0]
    displaced = apply_flex(local_loads)
    near = neighbours(jnp.concatenate([displaced, mode_block], axis=0))
    near_modes = near[load_count:]
    residual = displaced.astype(jnp.float32) - near[:load_count].astype(jnp.float32)
    rounded = residual.astype(jnp.bfloat16)
    payload = pack(weigh(rounded).astype(jnp.bfloat16))
    payload, mode_counts = lax.optimization_barrier((payload, mode_counts))
    stage = along_z(payload)

    all_ends = jnp.cumsum(mode_counts, axis=1)
    all_starts = all_ends - mode_counts
    own_first = column == 0
    counts = jnp.where(own_first, mode_counts[0], mode_counts[1])
    starts = jnp.where(own_first, all_starts[0], all_starts[1])
    padded = padded_inverse(coarse_inverse, starts, counts, 32 * row - column * column_width)

    column_of = jnp.stack([column, column, column, 1 - column])
    row_of = jnp.stack([row, row - 1, row + 1, row])
    chosen = jnp.logical_and(
        jnp.arange(rows)[None, None, :] == row_of[:, None, None],
        jnp.arange(2)[None, :, None] == column_of[:, None, None],
    )
    start_of = jnp.sum(jnp.where(chosen, all_starts[None], 0), axis=(1, 2))
    count_of = jnp.sum(jnp.where(chosen, mode_counts[None], 0), axis=(1, 2))
    base = column_of * column_width + start_of
    owner = jnp.minimum(base // 32, rows - 2)

    def place(chip):
        return (chip // (ny * nz)) * (ny * nz) + (chip % ny) * nz + (chip // ny) % nz

    info = jnp.stack([place(owner), place(owner + 1), base - 32 * owner, count_of], axis=1)
    info = info.reshape(-1).astype(jnp.int32)

    stage, padded, info, rounded = lax.optimization_barrier((stage, padded, info, rounded))
    smoothed = smooth(rounded)
    near_smoothed = neighbours(smoothed)
    blocks, near_smoothed = lax.optimization_barrier((across(stage), near_smoothed))
    first_sums = swapped_sum(coarse_product(padded, blocks))
    half_slots = first_sums.shape[0] // 2
    values = across(along_z(first_sums[:half_slots].astype(jnp.bfloat16)))
    direction, near_direction, moved = next_direction(
        info, values, mode_block, near_modes, smoothed, near_smoothed, exists
    )

    pushed = apply_flex(moved)
    curvature = load_dot(moved, pushed)
    partials = jnp.concatenate([load_dot(residual, direction), curvature])[None, :]
    pieces = in_pieces(partials)
    near_pushed = neighbours(pushed)
    near_pushed, pieces = lax.optimization_barrier((near_pushed, pieces))

    def difference(own, near):
        return own.astype(jnp.float32) - near.astype(jnp.float32)

    image = difference(pushed, near_pushed)
    image_high = lax.reduce_precision(image, 8, 7)
    image_low = (image - image_high).astype(jnp.bfloat16)
    image_weights = weigh(image_high.astype(jnp.bfloat16)) + weigh(image_low)
    payload = jnp.concatenate([pack(image_weights.astype(jnp.bfloat16)), pieces], axis=0)
    stage, late_pushed, late_near = lax.optimization_barrier(
        (summed_along_z(payload), pushed, near_pushed)
    )
    late_image = difference(late_pushed, late_near)
    image_smoothed = smooth(late_image.astype(jnp.bfloat16))
    residual_jump, image_jump = residual * factor, late_image * factor
    energies = (
        load_dot(residual_jump, smoothed),
        load_dot(residual_jump, image_smoothed) + load_dot(image_jump, smoothed),
        load_dot(image_jump, image_smoothed),
    )
    blocks, energies = lax.optimization_barrier((across(stage), energies))
    second_sums = swapped_sum(coarse_product(padded, blocks))
    totals = jnp.sum(second_sums[2 * half_slots :], axis=0)
    energy = totals[:64]
    size = energy / totals[64:]
    local_energy = energies[0] - size * (energies[1] - size * energies[2])

    packed = first_sums - jnp.tile(size, 2)[None, :] * second_sums[: 2 * half_slots]
    coarse_values = lax.reduce_precision(packed[:half_slots], 8, 7)
    coarse_energy = jnp.sum(coarse_values * packed[half_slots:], axis=0)
    partial = local_energy + 0.5 * (coarse_energy[:64] + coarse_energy[64:])
    partial = jnp.concatenate([partial, jnp.zeros_like(partial)])[None, :]
    payload = with_sum(coarse_values.astype(jnp.bfloat16), partial)
    payload, size = lax.optimization_barrier((payload, size))
    multipliers = size[:, None] * direction
    residual = residual - size[:, None] * image
    smoothed = smooth(residual.astype(jnp.bfloat16))
    stage, smoothed = lax.optimization_barrier((summed_along_z(payload), smoothed))
    near_smoothed = neighbours(smoothed)
    values = across(stage)
    sums = jnp.sum(values[:, nz * half_slots :, :].astype(jnp.float32), axis=(0, 1))[None, :]
    fresh = swapped_sum(sums)[0, :64]
    direction, near_direction, moved = next_direction(
        info,
        values,
        mode_block,
        near_modes,
        smoothed,
        near_smoothed,
        exists,
        (fresh / energy)[:, None],
        direction,
        near_direction,
    )

    pushed = apply_flex(moved)
    curvature = total(load_dot(moved, pushed)[None, :])[0]
    image = jump(pushed)
    size = (fresh / curvature)[:, None]
    multipliers = multipliers + size * direction
    residual = residual - size * image
    return (multipliers.astype(jnp.bfloat16)[None, None], residual.astype(jnp.bfloat16)[None, None])


def solution(mesh):
    split = Mesh(mesh.devices.reshape(XYZ + (2,)), WIDE + ("c",))
    blocks = P(WIDE, "c", None, None)
    return jax.shard_map(
        shards,
        mesh=split,
        in_specs=(blocks, blocks, blocks, blocks, P(WIDE, "c"), P()),
        out_specs=(blocks, blocks),
        check_vma=False,
    )
```

```python
import jax
import jax.numpy as jnp
from jax import lax
from jax.experimental import pallas as pl
from jax.experimental.pallas import tpu as pltpu
from jax.sharding import Mesh, PartitionSpec as P


XYZ = (4, 16, 4)
WIDE = ("x", "z", "y")
INTERPRET = False


def spread(values, axes):
    count = lax.axis_size(axes)
    copies = jnp.broadcast_to(values[None], (count,) + values.shape)
    return lax.all_to_all(copies, axes, 0, 0, tiled=False)


def along_z(block):
    return spread(block, "z").reshape(-1, block.shape[1])


def across(block):
    return spread(block, ("x", "y"))


def with_sum(block, partial):
    return jnp.concatenate([block, in_pieces(partial)], axis=0)


def summed_along_z(payload):
    stage = spread(payload, "z")
    rows = payload.shape[0] - 8
    sums = jnp.sum(stage[:, rows:, :].astype(jnp.float32), axis=(0, 1))[None, :]
    return with_sum(stage[:, :rows, :].reshape(-1, payload.shape[1]), sums)


def total(partial):
    stage = jnp.sum(spread(partial, ("x", "y", "c")), axis=0)
    return jnp.sum(spread(stage, "z"), axis=0)


def neighbours(values):
    _, width = values.shape
    face = width // 4
    rows = lax.axis_size(WIDE)
    column = lax.axis_index("c")
    down = [(i, i + 1) for i in range(rows - 1)]
    up = [(i + 1, i) for i in range(rows - 1)]
    north, south, west, east = (values[:, k * face : (k + 1) * face] for k in range(4))
    from_above = lax.ppermute(south, WIDE, down)
    from_below = lax.ppermute(north, WIDE, up)
    side = lax.ppermute(jnp.where(column == 0, east, west), "c", [(0, 1), (1, 0)])
    nothing = jnp.zeros_like(side)
    from_west = jnp.where(column == 1, side, nothing)
    from_east = jnp.where(column == 0, side, nothing)
    return jnp.concatenate([from_above, from_below, from_west, from_east], axis=1)


def jump(values):
    return values.astype(jnp.float32) - neighbours(values).astype(jnp.float32)


def pack(wide_rows):
    half = wide_rows.shape[0] // 2
    return jnp.concatenate([wide_rows[:half], wide_rows[half:]], axis=1)


def pad_kernel(first_ref, source_ref, block_ref, out_ref):
    rows, columns = block_ref.shape
    window = min(384, columns)
    chunks = out_ref.shape[1] // 128
    position = lax.broadcasted_iota(jnp.int32, (window, 128), 0)
    own_row = lax.broadcasted_iota(jnp.int32, (rows, window), 0) + first_ref[chunks]
    own_column = lax.broadcasted_iota(jnp.int32, (rows, window), 1)

    def step(chunk, carry):
        low = pl.multiple_of(first_ref[chunk] * 128, 128)
        unit = jnp.where(own_column + low == own_row, 1.0, 0.0).astype(jnp.bfloat16)
        part = jnp.concatenate([block_ref[:, pl.ds(low, window)], unit], axis=0)
        target = pl.multiple_of(chunk * 128, 128)
        for half in range(2):
            hot = jnp.where(position == source_ref[half, chunk] - low, 1.0, 0.0).astype(jnp.bfloat16)
            chosen = jnp.dot(part, hot, preferred_element_type=jnp.float32)
            out_ref[2 * half * rows : 2 * (half + 1) * rows, pl.ds(target, 128)] = chosen.astype(
                jnp.bfloat16
            )
        return carry

    lax.fori_loop(0, chunks, step, 0)


def padded_inverse(block, starts, counts, own_first):
    rows, columns = block.shape
    subdomains = counts.shape[0]
    slots = 32
    half_slots = slots // 2
    rank = jnp.arange(slots, dtype=jnp.int32)
    source = jnp.where(rank[None, :] < counts[:, None], starts[:, None] + rank[None, :], -1)
    chunks = subdomains * half_slots // 128
    source = source.reshape(subdomains, 2, half_slots).transpose(1, 0, 2).reshape(2, chunks, 1, 128)
    window = min(384, columns)
    first = jnp.minimum(starts.reshape(chunks, -1)[:, 0] // 128, (columns - window) // 128)
    first = jnp.concatenate([first, own_first[None]])
    return pl.pallas_call(
        pad_kernel,
        out_shape=jax.ShapeDtypeStruct((4 * rows, subdomains * half_slots), jnp.bfloat16),
        in_specs=[
            pl.BlockSpec(memory_space=pltpu.SMEM),
            pl.BlockSpec(memory_space=pltpu.VMEM),
            pl.BlockSpec(memory_space=pltpu.VMEM),
        ],
        out_specs=pl.BlockSpec(memory_space=pltpu.VMEM),
        interpret=INTERPRET,
        compiler_params=pltpu.CompilerParams(vmem_limit_bytes=8 << 20),
        name="pad_inverse",
    )(first, source, block)


def product_kernel(padded_ref, blocks_ref, out_ref):
    nx, nz, ny = XYZ
    rows = padded_ref.shape[0] // 4
    half = rows // 2
    length = nz * ny * half
    result = jnp.zeros((4 * rows, 128), jnp.float32)
    for x in range(nx):
        order = [(x * ny + y, z * half) for z in range(nz) for y in range(ny)]
        part = jnp.concatenate([blocks_ref[p, r : r + half, :] for p, r in order], axis=0)
        result += jnp.dot(
            padded_ref[:, x * length : (x + 1) * length], part, preferred_element_type=jnp.float32
        )
    joined = result[: 2 * rows] + pltpu.roll(result[2 * rows :], 64, 1)
    lane = lax.broadcasted_iota(jnp.int32, (half, 128), 1)
    for k in range(2):
        low = joined[2 * k * half : (2 * k + 1) * half]
        high = joined[(2 * k + 1) * half : (2 * k + 2) * half]
        out_ref[k * half : (k + 1) * half, :] = jnp.where(lane < 64, low, pltpu.roll(high, 64, 1))
    if out_ref.shape[0] > rows:
        sums = jnp.zeros((8, 128), jnp.float32)
        for p in range(blocks_ref.shape[0]):
            sums += blocks_ref[p, nz * half : nz * half + 8, :].astype(jnp.float32)
        out_ref[rows : rows + 8, :] = sums


def coarse_product(padded, blocks):
    rows = padded.shape[0] // 4
    return pl.pallas_call(
        product_kernel,
        out_shape=jax.ShapeDtypeStruct((rows + blocks.shape[1] - XYZ[1] * (rows // 2), 128), jnp.float32),
        in_specs=[pl.BlockSpec(memory_space=pltpu.VMEM)] * 2,
        out_specs=pl.BlockSpec(memory_space=pltpu.VMEM),
        interpret=INTERPRET,
        compiler_params=pltpu.CompilerParams(vmem_limit_bytes=8 << 20),
        name="coarse_product",
    )(padded, blocks)


def in_pieces(values):
    rest = values
    pieces = []
    for _ in range(3):
        piece = lax.reduce_precision(rest, 8, 7)
        pieces.append(piece)
        rest = rest - piece
    pieces.append(jnp.zeros((8 - len(pieces), values.shape[1]), jnp.float32))
    return jnp.concatenate(pieces, axis=0).astype(jnp.bfloat16)


def swapped_sum(partial):
    return partial + lax.ppermute(partial, "c", [(0, 1), (1, 0)])


def direction_kernel(info_ref, blocks_ref, *refs):
    modes_ref, near_modes_ref, smoothed_ref, near_smoothed_ref, exists_ref = refs[:5]
    out_ref, near_ref, moved_ref = refs[-3:]
    slots, width = modes_ref.shape
    load_count = out_ref.shape[0]
    face = width // 4
    half_slots = slots // 2
    rank = lax.broadcasted_iota(jnp.int32, (slots, slots), 0)
    column = lax.broadcasted_iota(jnp.int32, (slots, slots), 1)

    def chip_block(chip):
        start = pl.multiple_of((chip % XYZ[1]) * half_slots, half_slots)
        return blocks_ref[chip // XYZ[1], pl.ds(start, half_slots), :]

    def lifted(which, rows):
        window = jnp.concatenate(
            [chip_block(info_ref[4 * which]), chip_block(info_ref[4 * which + 1])], axis=0
        )
        offset = info_ref[4 * which + 2] + rank
        row = (offset // slots) * half_slots + offset % half_slots
        second = (offset // half_slots) % 2 == 1
        hit = jnp.logical_and(row == column, rank < info_ref[4 * which + 3])
        low = jnp.where(jnp.logical_and(hit, jnp.logical_not(second)), 1.0, 0.0)
        high = jnp.where(jnp.logical_and(hit, second), 1.0, 0.0)
        picked = jnp.dot(
            low.astype(jnp.bfloat16), window, preferred_element_type=jnp.float32
        ) + pltpu.roll(
            jnp.dot(high.astype(jnp.bfloat16), window, preferred_element_type=jnp.float32), 64, 1
        )
        result = lax.dot_general(
            picked.astype(jnp.bfloat16),
            rows,
            (((0,), (0,)), ((), ())),
            preferred_element_type=jnp.float32,
        )
        return result[:load_count]

    local = smoothed_ref[...].astype(jnp.float32) - near_smoothed_ref[...].astype(jnp.float32)
    direction = local + lifted(0, modes_ref[...])
    near_lifted = jnp.concatenate(
        [
            lifted(1, near_modes_ref[:, :face]),
            lifted(2, near_modes_ref[:, face : 2 * face]),
            lifted(3, near_modes_ref[:, 2 * face :]),
        ],
        axis=1,
    )
    near = near_lifted - exists_ref[...] * local
    if len(refs) > 8:
        ratio_ref, previous_ref, near_previous_ref = refs[5:8]
        ratio = ratio_ref[...]
        direction += ratio * previous_ref[...]
        near += ratio * near_previous_ref[...]
    out_ref[...] = direction
    near_ref[...] = near
    moved_ref[...] = (
        direction.astype(jnp.bfloat16).astype(jnp.float32)
        - near.astype(jnp.bfloat16).astype(jnp.float32)
    ).astype(jnp.bfloat16)


def next_direction(info, blocks, modes, near_modes, smoothed, near_smoothed, exists, *previous):
    rest = (modes, near_modes, smoothed, near_smoothed, exists) + previous
    shape = smoothed.shape
    in_vmem = pl.BlockSpec(memory_space=pltpu.VMEM)
    return pl.pallas_call(
        direction_kernel,
        out_shape=(
            jax.ShapeDtypeStruct(shape, jnp.float32),
            jax.ShapeDtypeStruct(shape, jnp.float32),
            jax.ShapeDtypeStruct(shape, jnp.bfloat16),
        ),
        in_specs=[pl.BlockSpec(memory_space=pltpu.SMEM)] + [in_vmem] * (1 + len(rest)),
        out_specs=(in_vmem,) * 3,
        interpret=INTERPRET,
        compiler_params=pltpu.CompilerParams(vmem_limit_bytes=(56 if previous else 8) << 20),
        name="next_direction",
    )(info, blocks, *rest)


def shards(loads, flexibility, dirichlet, modes, coarse_inverse, mode_counts):
    local_loads = loads[0, 0]
    flex_block = flexibility[0, 0]
    precond_block = dirichlet[0, 0]
    mode_block = modes[0, 0]
    _, nz, ny = XYZ
    rows = lax.axis_size(WIDE)
    row = lax.axis_index(WIDE)
    column = lax.axis_index("c")
    column_width = coarse_inverse.shape[1]
    face = local_loads.shape[1] // 4

    has_neighbour = jnp.stack([row > 0, row < rows - 1, column == 1, column == 0])
    exists = jnp.repeat(jnp.where(has_neighbour, 1.0, 0.0), face)[None, :]
    factor = 1.0 + exists

    def weigh(rounded):
        return lax.dot_general(
            mode_block, rounded, (((1,), (1,)), ((), ())), preferred_element_type=jnp.float32
        )

    def smooth(rounded):
        inner = (rounded.astype(jnp.float32) * factor).astype(jnp.bfloat16)
        return jnp.dot(inner, precond_block, preferred_element_type=jnp.float32).astype(
            jnp.bfloat16
        )

    def apply_flex(values):
        return jnp.dot(values, flex_block, preferred_element_type=jnp.float32).astype(jnp.bfloat16)

    def load_dot(left, right):
        return jnp.sum(left.astype(jnp.float32) * right.astype(jnp.float32), axis=1)

    load_count = local_loads.shape[0]
    displaced = apply_flex(local_loads)
    near = neighbours(jnp.concatenate([displaced, mode_block], axis=0))
    near_modes = near[load_count:]
    residual = displaced.astype(jnp.float32) - near[:load_count].astype(jnp.float32)
    rounded = residual.astype(jnp.bfloat16)
    payload = pack(weigh(rounded).astype(jnp.bfloat16))
    payload, mode_counts = lax.optimization_barrier((payload, mode_counts))
    stage = along_z(payload)

    all_ends = jnp.cumsum(mode_counts, axis=1)
    all_starts = all_ends - mode_counts
    own_first = column == 0
    counts = jnp.where(own_first, mode_counts[0], mode_counts[1])
    starts = jnp.where(own_first, all_starts[0], all_starts[1])
    padded = padded_inverse(coarse_inverse, starts, counts, 32 * row - column * column_width)

    column_of = jnp.stack([column, column, column, 1 - column])
    row_of = jnp.stack([row, row - 1, row + 1, row])
    chosen = jnp.logical_and(
        jnp.arange(rows)[None, None, :] == row_of[:, None, None],
        jnp.arange(2)[None, :, None] == column_of[:, None, None],
    )
    start_of = jnp.sum(jnp.where(chosen, all_starts[None], 0), axis=(1, 2))
    count_of = jnp.sum(jnp.where(chosen, mode_counts[None], 0), axis=(1, 2))
    base = column_of * column_width + start_of
    owner = jnp.minimum(base // 32, rows - 2)

    def place(chip):
        return (chip // (ny * nz)) * (ny * nz) + (chip % ny) * nz + (chip // ny) % nz

    info = jnp.stack([place(owner), place(owner + 1), base - 32 * owner, count_of], axis=1)
    info = info.reshape(-1).astype(jnp.int32)

    stage, padded, info = lax.optimization_barrier((stage, padded, info))
    first_sums = swapped_sum(coarse_product(padded, across(stage)))
    half_slots = first_sums.shape[0] // 2
    stage = along_z(first_sums[:half_slots].astype(jnp.bfloat16))
    stage, rounded = lax.optimization_barrier((stage, rounded))
    smoothed = smooth(rounded)
    near_smoothed = neighbours(smoothed)
    direction, near_direction, moved = next_direction(
        info, across(stage), mode_block, near_modes, smoothed, near_smoothed, exists
    )

    pushed = apply_flex(moved)
    curvature = load_dot(moved, pushed)
    partials = jnp.concatenate([load_dot(residual, direction), curvature])[None, :]
    pieces = in_pieces(partials)
    near_pushed = neighbours(pushed)
    near_pushed, pieces = lax.optimization_barrier((near_pushed, pieces))

    def difference(own, near):
        return own.astype(jnp.float32) - near.astype(jnp.float32)

    image = difference(pushed, near_pushed)
    image_high = lax.reduce_precision(image, 8, 7)
    image_low = (image - image_high).astype(jnp.bfloat16)
    image_weights = weigh(image_high.astype(jnp.bfloat16)) + weigh(image_low)
    payload = jnp.concatenate([pack(image_weights.astype(jnp.bfloat16)), pieces], axis=0)
    products = coarse_product(padded, across(summed_along_z(payload)))
    products, late_pushed, late_near = lax.optimization_barrier((products, pushed, near_pushed))
    late_image = difference(late_pushed, late_near)
    image_smoothed = smooth(late_image.astype(jnp.bfloat16))
    residual_jump, image_jump = residual * factor, late_image * factor
    energies = (
        load_dot(residual_jump, smoothed),
        load_dot(residual_jump, image_smoothed) + load_dot(image_jump, smoothed),
        load_dot(image_jump, image_smoothed),
    )
    second_sums = swapped_sum(products)
    totals = jnp.sum(second_sums[2 * half_slots :], axis=0)
    energy = totals[:64]
    size = energy / totals[64:]
    local_energy = energies[0] - size * (energies[1] - size * energies[2])

    packed = first_sums - jnp.tile(size, 2)[None, :] * second_sums[: 2 * half_slots]
    coarse_values = lax.reduce_precision(packed[:half_slots], 8, 7)
    coarse_energy = jnp.sum(coarse_values * packed[half_slots:], axis=0)
    partial = local_energy + 0.5 * (coarse_energy[:64] + coarse_energy[64:])
    partial = jnp.concatenate([partial, jnp.zeros_like(partial)])[None, :]
    payload = with_sum(coarse_values.astype(jnp.bfloat16), partial)
    payload, size = lax.optimization_barrier((payload, size))
    multipliers = size[:, None] * direction
    residual = residual - size[:, None] * image
    smoothed = smooth(residual.astype(jnp.bfloat16))
    stage, smoothed = lax.optimization_barrier((summed_along_z(payload), smoothed))
    near_smoothed = neighbours(smoothed)
    values = across(stage)
    sums = jnp.sum(values[:, nz * half_slots :, :].astype(jnp.float32), axis=(0, 1))[None, :]
    fresh = swapped_sum(sums)[0, :64]
    direction, near_direction, moved = next_direction(
        info,
        values,
        mode_block,
        near_modes,
        smoothed,
        near_smoothed,
        exists,
        (fresh / energy)[:, None],
        direction,
        near_direction,
    )

    pushed = apply_flex(moved)
    curvature = total(load_dot(moved, pushed)[None, :])[0]
    image = jump(pushed)
    size = (fresh / curvature)[:, None]
    multipliers = multipliers + size * direction
    residual = residual - size * image
    return (multipliers.astype(jnp.bfloat16)[None, None], residual.astype(jnp.bfloat16)[None, None])


def solution(mesh):
    split = Mesh(mesh.devices.reshape(XYZ + (2,)), WIDE + ("c",))
    blocks = P(WIDE, "c", None, None)
    return jax.shard_map(
        shards,
        mesh=split,
        in_specs=(blocks, blocks, blocks, blocks, P(WIDE, "c"), P()),
        out_specs=(blocks, blocks),
        check_vma=False,
    )
```
